512 devices in a mesh: dp: 16 (over z), ctx: 32 (over y, x, core).
Axes of the slice: x: 4, y: 4, z: 16, core: 2. Of those that a mesh axis runs over, the one named last changes fastest.
Arguments:
- queries: bfloat16 [16, 4096, 4096], P('dp', 'ctx'), may hold values from -216 to 216
- keys: bfloat16 [16, 4096, 1024], P('dp', 'ctx'), may hold values from -6 to 6
- values: bfloat16 [16, 4096, 1024], P('dp', 'ctx'), may hold values from -6 to 6
- out_grad: bfloat16 [16, 4096, 4096], P('dp', 'ctx'), may hold values from -6 to 6
- block_mask: int32 [32, 32, 32], replicated, may hold values from 0 to 1, as said below
Outputs:
- query_grad: bfloat16 [16, 4096, 4096], P('dp', 'ctx')
- key_grad: bfloat16 [16, 4096, 1024], P('dp', 'ctx')
- value_grad: bfloat16 [16, 4096, 1024], P('dp', 'ctx')
- z_loss: float32 [32], P('ctx')
The draws below stay inside these ranges and needn't reach their ends.
Inputs may be any that keep to these rules, and one draw needn't show every extreme that they name: block_mask[h, a, b] is 1 only where b <= a; block_mask[h, a, a] = 1 and block_mask[h, a, 0] = 1 for every head h and query block a.
All inputs are finite; a program needn't handle non-finite values.
Results may differ from the reference program's by a relative error of at most 0.014.
Values may be sent and summed in bfloat16 or wider, within the bound.
No kernel may reach another device: no remote copies, remote signals or barrier semaphores. Data moves between devices by JAX's collectives and lax.ppermute only.
A program may use at most 128 MiB of HBM per device.

```python
import jax
import jax.numpy as jnp
from jax import lax

H = 32
KVH = 8
HD = 128
BLK = 128
SEQ = 4096
BATCH = 16


def query_key_pair(key):
    base = jax.random.fold_in(key, 101)
    query_key, key_key = jax.random.split(base, 2)
    key_raw = jnp.clip(jax.random.normal(key_key, (BATCH, SEQ, KVH, HD), jnp.float32), -6.0, 6.0)
    query_raw = jnp.clip(jax.random.normal(query_key, (BATCH, SEQ, H, HD), jnp.float32), -6.0, 6.0)
    key_out = key_raw
    query_out = query_raw
    return (query_out.reshape(BATCH, SEQ, H * HD), key_out.reshape(BATCH, SEQ, KVH * HD))


def draw_queries(key, part):
    return query_key_pair(key)[0].astype(jnp.bfloat16)


def draw_keys(key, part):
    return query_key_pair(key)[1].astype(jnp.bfloat16)


def draw_block_mask(key, part):
    block_total = SEQ // BLK
    level_key, column_key, slash_key = jax.random.split(jax.random.fold_in(key, 211), 3)
    level = jax.random.randint(level_key, (H, 1, 1), 1, 17)
    vertical = jax.random.randint(column_key, (H, 1, block_total), 0, 96) < level
    slash = jax.random.randint(slash_key, (H, block_total), 0, 384) < level[:, :, 0]
    query_block = jnp.arange(block_total)[:, None]
    key_block = jnp.arange(block_total)[None, :]
    offset = jnp.clip(query_block - key_block, 0, block_total - 1)
    slash_on = slash[:, offset]
    active = vertical | slash_on | (key_block == 0) | (key_block == query_block)
    active = active & (key_block <= query_block)
    return active.astype(jnp.int32)


def level_of(own_key, shape, cuts, smallest, high):
    factor_of = 1.0
    for dim, parts in cuts:
        draws = jax.random.uniform(jax.random.fold_in(jax.random.fold_in(own_key, 6), dim), (parts,), jnp.float32, smallest / len(cuts), high / len(cuts))
        factor_of = factor_of * jnp.repeat(jnp.exp(draws), shape[dim] // parts).reshape((-1,) + (1,) * (len(shape) - 1 - dim))
    return factor_of


def noise(own_key, dims, scale, bound, cuts=(), kind=jnp.bfloat16):
    result = jax.random.normal(own_key, dims, jnp.float32) * scale
    if len(cuts) > 0:
        result = level_of(own_key, dims, cuts, -0.22, 0.18) * result
    return jnp.clip(result, min=-bound, max=bound).astype(kind)


def setup_inputs(seed: int = 0) -> dict:
    arg_keys = jax.random.split(jax.random.key(seed), 6)
    return {
        "queries": draw_queries(jax.random.fold_in(arg_keys[5], 71), 0),
        "keys": draw_keys(jax.random.fold_in(arg_keys[5], 71), 0),
        "values": noise(arg_keys[2], (BATCH, SEQ, KVH * HD), 1.0, 6.0, ((0, 16), (1, 32))),
        "out_grad": noise(arg_keys[3], (BATCH, SEQ, H * HD), 1.0, 6.0, ((0, 16), (1, 32))),
        "block_mask": draw_block_mask(jax.random.fold_in(arg_keys[5], 71), 0),
    }


ZLOSS = 0.05
NEG = -1e30


def head_group(query_g, grad_g, key_g, value_g, mask_g):
    group_size = H // KVH
    tile_rows = 4 * BLK
    tile_count = SEQ // tile_rows
    softmax_scale = HD ** -0.5
    key_f32 = key_g.astype(jnp.float32)
    value_f32 = value_g.astype(jnp.float32)
    key_acc = jnp.zeros((SEQ, HD), jnp.float32)
    value_acc = jnp.zeros((SEQ, HD), jnp.float32)
    dq_heads = []
    z_heads = []
    for member in range(group_size):
        dq_tiles = []
        z_sum = jnp.zeros((), jnp.float32)
        for tile_pos in range(tile_count):
            first_row = tile_pos * tile_rows
            key_span = first_row + tile_rows
            q_tile = query_g[member, first_row:key_span].astype(jnp.float32)
            g_tile = grad_g[member, first_row:key_span].astype(jnp.float32)
            keys_here = key_f32[:key_span]
            values_here = value_f32[:key_span]
            scores = jnp.dot(q_tile, keys_here.T, precision=lax.Precision.HIGHEST) * softmax_scale
            tile_blocks = mask_g[member, 4 * tile_pos:4 * tile_pos + 4, :key_span // BLK]
            block_on = jnp.repeat(jnp.repeat(tile_blocks, BLK, axis=0), BLK, axis=1) > 0
            query_pos = first_row + jnp.arange(tile_rows)
            key_pos = jnp.arange(key_span)
            allowed = block_on & (key_pos[None, :] <= query_pos[:, None])
            row_max = jnp.max(jnp.where(allowed, scores, NEG), axis=1)
            row_sum = jnp.sum(jnp.where(allowed, jnp.exp(scores - row_max[:, None]), 0.0), axis=1)
            log_norm = row_max + jnp.log(row_sum)
            probs = jnp.where(allowed, jnp.exp(scores - log_norm[:, None]), 0.0)
            probs_low = probs.astype(jnp.bfloat16).astype(jnp.float32)
            attn_out = jnp.dot(probs_low, values_here, precision=lax.Precision.HIGHEST).astype(jnp.bfloat16)
            row_delta = jnp.sum(g_tile * attn_out.astype(jnp.float32), axis=1)
            prob_grad = jnp.dot(g_tile, values_here.T, precision=lax.Precision.HIGHEST)
            dscore = (probs * (prob_grad - row_delta[:, None] + 2.0 * ZLOSS * log_norm[:, None])).astype(jnp.bfloat16).astype(jnp.float32)
            dq_tile = softmax_scale * jnp.dot(dscore, keys_here, precision=lax.Precision.HIGHEST)
            dq_tiles.append(dq_tile.astype(jnp.bfloat16))
            key_acc = key_acc.at[:key_span].add(softmax_scale * jnp.dot(dscore.T, q_tile, precision=lax.Precision.HIGHEST))
            value_acc = value_acc.at[:key_span].add(jnp.dot(probs_low.T, g_tile, precision=lax.Precision.HIGHEST))
            z_sum = z_sum + jnp.sum(log_norm * log_norm)
        dq_heads.append(jnp.concatenate(dq_tiles, axis=0))
        z_heads.append(z_sum)
    return jnp.stack(dq_heads), key_acc.astype(jnp.bfloat16), value_acc.astype(jnp.bfloat16), jnp.stack(z_heads)


def reference(queries, keys, values, out_grad, block_mask):
    group_size = H // KVH
    block_total = SEQ // BLK
    query_g = queries.reshape(BATCH, SEQ, KVH, group_size, HD).transpose(0, 2, 3, 1, 4).reshape(BATCH * KVH, group_size, SEQ, HD)
    grad_g = out_grad.reshape(BATCH, SEQ, KVH, group_size, HD).transpose(0, 2, 3, 1, 4).reshape(BATCH * KVH, group_size, SEQ, HD)
    key_g = keys.reshape(BATCH, SEQ, KVH, HD).transpose(0, 2, 1, 3).reshape(BATCH * KVH, SEQ, HD)
    value_g = values.reshape(BATCH, SEQ, KVH, HD).transpose(0, 2, 1, 3).reshape(BATCH * KVH, SEQ, HD)
    mask_g = jnp.tile(block_mask.reshape(KVH, group_size, block_total, block_total), (BATCH, 1, 1, 1))

    def run_group(pieces):
        return head_group(pieces[0], pieces[1], pieces[2], pieces[3], pieces[4])

    dq_all, dk_all, dv_all, z_all = lax.map(run_group, (query_g, grad_g, key_g, value_g, mask_g))
    query_grad = dq_all.reshape(BATCH, KVH, group_size, SEQ, HD).transpose(0, 3, 1, 2, 4).reshape(BATCH, SEQ, H * HD)
    key_grad = dk_all.reshape(BATCH, KVH, SEQ, HD).transpose(0, 2, 1, 3).reshape(BATCH, SEQ, KVH * HD)
    value_grad = dv_all.reshape(BATCH, KVH, SEQ, HD).transpose(0, 2, 1, 3).reshape(BATCH, SEQ, KVH * HD)
    z_loss = jnp.sum(z_all.reshape(BATCH, H), axis=0) * (ZLOSS / (BATCH * SEQ))
    return query_grad, key_grad, value_grad, z_loss
```

```python
import functools
import math

import jax
import jax.numpy as jnp
from jax import lax
from jax.experimental import pallas as pl
from jax.experimental.pallas import tpu as pltpu
from jax.sharding import PartitionSpec as P

H = 32
KVH = 8
HD = 128
BLK = 128
GRP = H // KVH

ZLOSS = 0.05
NEG = -1e30
LOG2E = 1.0 / math.log(2.0)
LN2 = math.log(2.0)
SCALE = HD ** (-0.5)

NT = (((1,), (1,)), ((), ()))


def attention_body(
    cols_ref, cnt_ref, steps_ref, edge_ref,
    qd_ref, kv_ref,
    dq_ref, dkv_ref, z_ref,
    e_s, dp_s, m_s, dk_s, dv_s, kt_s, dqt_s, z_s,
):
    row = pl.program_id(0)
    blocks = kv_ref.shape[0]

    @pl.when(row == 0)
    def _():
        dk_s[...] = jnp.zeros_like(dk_s)
        dv_s[...] = jnp.zeros_like(dv_s)
        z_s[...] = jnp.zeros_like(z_s)

        @pl.loop(0, blocks)
        def _(b):
            kt_s[b] = kv_ref[b, :, :HD].astype(jnp.float32).T.astype(jnp.bfloat16)

    qs = [qd_ref[0, :, j * HD : (j + 1) * HD] for j in range(GRP)]
    gs = [qd_ref[0, :, (GRP + j) * HD : (GRP + j + 1) * HD] for j in range(GRP)]
    q_all = jnp.concatenate(qs, axis=0)
    g_all = jnp.concatenate(gs, axis=0)

    def dot(a, b):
        return jnp.dot(a, b, preferred_element_type=jnp.float32)

    def dot_nt(a, b):
        return lax.dot_general(a, b, NT, preferred_element_type=jnp.float32)

    def pair(c1, c2):
        k = jnp.concatenate([kv_ref[c1, :, :HD], kv_ref[c2, :, :HD]], axis=0)
        v = jnp.concatenate([kv_ref[c1, :, HD:], kv_ref[c2, :, HD:]], axis=0)
        return k, v

    diag = edge_ref[row, 0]
    first_bias = jnp.where(edge_ref[row, 1] > 0, NEG, 0.0).astype(jnp.float32)
    k0, v0 = pair(0, diag)
    s_all = dot_nt(k0, q_all) * (SCALE * LOG2E)
    dp_all = dot_nt(v0, g_all)
    key_pos = lax.broadcasted_iota(jnp.int32, (BLK, BLK), 0)
    query_pos = lax.broadcasted_iota(jnp.int32, (BLK, BLK), 1)
    causal = key_pos <= query_pos
    state = []
    for j in range(GRP):
        cut = slice(j * BLK, (j + 1) * BLK)
        s = jnp.concatenate(
            [s_all[:BLK, cut] + first_bias, jnp.where(causal, s_all[BLK:, cut], NEG)], axis=0
        )
        dp = dp_all[:, cut]
        m = jnp.max(s, axis=0, keepdims=True)
        e = jnp.exp2(s - m)
        e_s[0, j] = e
        dp_s[0, j] = dp
        m_s[0, j] = jnp.broadcast_to(m, (8, BLK))
        state += [m, jnp.sum(e, axis=0, keepdims=True), jnp.sum(e * dp, axis=0, keepdims=True)]

    def entry(t, j):
        slot = 2 * (t - 1)
        c1 = cols_ref[row, j * blocks + slot]
        c2 = cols_ref[row, j * blocks + slot + 1]
        return slot, c1, c2

    def forward(t, state):
        out = []
        for j in range(GRP):
            m, l, u = state[3 * j : 3 * j + 3]
            slot, c1, c2 = entry(t, j)
            n = cnt_ref[row, j]
            b1 = jnp.where(slot < n, 0.0, NEG).astype(jnp.float32)
            b2 = jnp.where(slot + 1 < n, 0.0, NEG).astype(jnp.float32)
            k, v = pair(c1, c2)
            s = dot_nt(k, qs[j]) * (SCALE * LOG2E)
            s = jnp.concatenate([s[:BLK] + b1, s[BLK:] + b2], axis=0)
            dp = dot_nt(v, gs[j])
            m_new = jnp.maximum(m, jnp.max(s, axis=0, keepdims=True))
            e = jnp.exp2(s - m_new)
            alpha = jnp.exp2(m - m_new)
            e_s[t, j] = e
            dp_s[t, j] = dp
            m_s[t, j] = jnp.broadcast_to(m_new, (8, BLK))
            out += [
                m_new,
                l * alpha + jnp.sum(e, axis=0, keepdims=True),
                u * alpha + jnp.sum(e * dp, axis=0, keepdims=True),
            ]
        return tuple(out)

    steps = steps_ref[row, 0]
    state = lax.fori_loop(1, steps, forward, tuple(state))

    top, inv, pull = [], [], []
    for j in range(GRP):
        m, l, u = state[3 * j : 3 * j + 3]
        inv_l = 1.0 / l
        log_norm = m * LN2 + jnp.log(l)
        top.append(m)
        inv.append(inv_l)
        pull.append((2.0 * ZLOSS) * log_norm - u * inv_l)
        z_s[j : j + 1, :] += log_norm * log_norm

    def weights(t, j):
        factor = jnp.exp2(m_s[t, j][:1] - top[j]) * inv[j]
        probs = e_s[t, j] * factor
        dscore = probs * (dp_s[t, j] + pull[j])
        return probs.astype(jnp.bfloat16), dscore.astype(jnp.bfloat16)

    first = [weights(0, j) for j in range(GRP)]
    p_all = jnp.concatenate([w[0] for w in first], axis=1)
    d_all = jnp.concatenate([w[1] for w in first], axis=1)
    dk = dot(d_all, q_all)
    dv = dot(p_all, g_all)
    dk_s[0] += dk[:BLK]
    dv_s[0] += dv[:BLK]
    dk_s[diag] += dk[BLK:]
    dv_s[diag] += dv[BLK:]
    kt = jnp.concatenate([kt_s[0], kt_s[diag]], axis=1)
    dqt = dot(kt, d_all)
    for j in range(GRP):
        dqt_s[j] = dqt[:, j * BLK : (j + 1) * BLK]

    @pl.loop(1, steps)
    def _(t):
        for j in range(GRP):
            _, c1, c2 = entry(t, j)
            p_low, d_low = weights(t, j)
            dk = dot(d_low, qs[j])
            dv = dot(p_low, gs[j])
            kt = jnp.concatenate([kt_s[c1], kt_s[c2]], axis=1)
            dqt_s[j] += dot(kt, d_low)
            dk_s[c1] += dk[:BLK]
            dv_s[c1] += dv[:BLK]
            dk_s[c2] += dk[BLK:]
            dv_s[c2] += dv[BLK:]

    for j in range(GRP):
        dq_ref[0, :, j * HD : (j + 1) * HD] = (dqt_s[j] * SCALE).T.astype(jnp.bfloat16)

    @pl.when(row == pl.num_programs(0) - 1)
    def _():
        dkv_ref[:, :, :HD] = (dk_s[...] * SCALE).astype(jnp.bfloat16)
        dkv_ref[:, :, HD:] = dv_s[...].astype(jnp.bfloat16)
        z_ref[...] = z_s[...]


def attention(qd, kv, cols, cnt, steps, edge):
    rows = qd.shape[0]
    blocks = kv.shape[0]
    max_steps = blocks // 2
    return pl.pallas_call(
        attention_body,
        out_shape=(
            jax.ShapeDtypeStruct((rows, BLK, GRP * HD), jnp.bfloat16),
            jax.ShapeDtypeStruct((blocks, BLK, 2 * HD), jnp.bfloat16),
            jax.ShapeDtypeStruct((8, BLK), jnp.float32),
        ),
        grid_spec=pltpu.PrefetchScalarGridSpec(
            num_scalar_prefetch=4,
            grid=(rows,),
            in_specs=[
                pl.BlockSpec((1, BLK, 2 * GRP * HD), lambda i, *_: (i, 0, 0)),
                pl.BlockSpec((blocks, BLK, 2 * HD), lambda i, *_: (0, 0, 0)),
            ],
            out_specs=[
                pl.BlockSpec((1, BLK, GRP * HD), lambda i, *_: (i, 0, 0)),
                pl.BlockSpec((blocks, BLK, 2 * HD), lambda i, *_: (0, 0, 0)),
                pl.BlockSpec((8, BLK), lambda i, *_: (0, 0)),
            ],
            scratch_shapes=[
                pltpu.VMEM((max_steps, GRP, 2 * BLK, BLK), jnp.float32),
                pltpu.VMEM((max_steps, GRP, 2 * BLK, BLK), jnp.float32),
                pltpu.VMEM((max_steps, GRP, 8, BLK), jnp.float32),
                pltpu.VMEM((blocks, BLK, HD), jnp.float32),
                pltpu.VMEM((blocks, BLK, HD), jnp.float32),
                pltpu.VMEM((blocks, HD, BLK), jnp.bfloat16),
                pltpu.VMEM((GRP, HD, BLK), jnp.float32),
                pltpu.VMEM((8, BLK), jnp.float32),
            ],
        ),
        compiler_params=pltpu.CompilerParams(
            dimension_semantics=("arbitrary",), vmem_limit_bytes=44 << 20
        ),
        cost_estimate=pl.CostEstimate(
            flops=40_000_000_000, transcendentals=4_000_000, bytes_accessed=9_000_000
        ),
        name="block_attention",
    )(cols, cnt, steps, edge, qd, kv)


def work_lists(mask, part, parts):
    rows, blocks = mask.shape[1:]
    mask = jnp.transpose(mask, (1, 0, 2))
    col = jnp.arange(blocks, dtype=jnp.int32)
    own = jnp.arange(rows, dtype=jnp.int32) * parts + part
    other = (mask > 0) & (col > 0)[None, None, :] & (col[None, :] != own[:, None])[:, None, :]
    other = other.astype(jnp.int32)
    before = (col[None, :] < col[:, None]).astype(jnp.int32)
    rank = jnp.sum(other[:, :, None, :] * before[None, None], axis=3)
    place = (col % parts) * rows + col // parts
    hit = (rank[:, :, None, :] == col[None, None, :, None]) & (other[:, :, None, :] > 0)
    cols = jnp.sum(jnp.where(hit, place[None, None, None, :], 0), axis=3)
    cnt = jnp.sum(other, axis=2)
    steps = 1 + (jnp.max(cnt, axis=1) + 1) // 2
    edge = jnp.stack([part * rows + jnp.arange(rows, dtype=jnp.int32), (own == 0).astype(jnp.int32)], axis=1)
    return cols.reshape(rows, GRP * blocks), cnt, steps[:, None], edge


def body(queries, keys, values, out_grad, block_mask):
    tok = queries.shape[1]
    ctx = lax.axis_size("ctx")
    dps = lax.axis_size("dp")
    parts = ctx // KVH
    blocks = block_mask.shape[1]
    rows = blocks // parts
    me = lax.axis_index("ctx")
    kv_head, part = me // parts, me % parts
    spread = [[u * parts + r for u in range(KVH)] for r in range(parts)]
    quad = [[u * parts + r for r in range(parts)] for u in range(KVH)]
    wide = [[d * ctx + u * parts + r for d in range(dps) for r in range(parts)] for u in range(KVH)]

    def heads_first(*arrays):
        return jnp.concatenate([a[0].reshape(tok, KVH, -1) for a in arrays], axis=2).transpose(1, 0, 2)

    def exchange(a):
        return lax.all_to_all(a, "ctx", 0, 0, axis_index_groups=spread, tiled=True)

    kv_part = exchange(heads_first(keys, values))
    kv = lax.all_gather(kv_part, "ctx", axis=0, axis_index_groups=quad, tiled=True)
    qd = exchange(heads_first(queries, out_grad))

    mask = lax.dynamic_slice(
        block_mask.reshape(H, rows, parts, blocks), (kv_head * GRP, 0, part, 0), (GRP, rows, 1, blocks)
    )[:, :, 0]
    cols, cnt, steps, edge = work_lists(mask, part, parts)
    dq, dkv, z = attention(qd, kv, cols, cnt, steps, edge)

    z_send = jnp.tile(z[:GRP], (dps, 1))
    z_back = lax.all_to_all(z_send, ("dp", "ctx"), 0, 0, axis_index_groups=wide, tiled=True)
    dkv_part = lax.psum_scatter(dkv, "ctx", scatter_dimension=0, axis_index_groups=quad, tiled=True)
    query_grad = exchange(dq).transpose(1, 0, 2).reshape(1, tok, H * HD)
    dkv_back = exchange(dkv_part).transpose(1, 0, 2)
    key_grad = dkv_back[:, :, :HD].reshape(1, tok, KVH * HD)
    value_grad = dkv_back[:, :, HD:].reshape(1, tok, KVH * HD)
    z_own = jnp.sum(z_back)[None] * (ZLOSS / (dps * blocks * BLK))
    return query_grad, key_grad, value_grad, z_own


def solution(mesh):
    return jax.shard_map(
        body,
        mesh=mesh,
        in_specs=(
            P("dp", "ctx", None),
            P("dp", "ctx", None),
            P("dp", "ctx", None),
            P("dp", "ctx", None),
            P(),
        ),
        out_specs=(P("dp", "ctx", None), P("dp", "ctx", None), P("dp", "ctx", None), P("ctx")),
        check_vma=False,
    )
```

```python
import math

import jax
import jax.numpy as jnp
from jax import lax
from jax.experimental import pallas as pl
from jax.experimental.pallas import tpu as pltpu
from jax.sharding import PartitionSpec as P

H = 32
KVH = 8
HD = 128
BLK = 128
GRP = H // KVH
PARTS = 4

ZLOSS = 0.05
NEG = -1e30
LOG2E = 1.0 / math.log(2.0)
LN2 = math.log(2.0)
SCALE = HD ** (-0.5)

NT = (((1,), (1,)), ((), ()))


def attention_body(
    cols_ref, cnt_ref, steps_ref, edge_ref,
    qd_ref, kv_ref,
    dq_ref, dkv_ref, z_ref,
    e_s, dp_s, m_s, dk_s, dv_s, kt_s, dqt_s, z_s,
):
    row = pl.program_id(0)
    blocks = kv_ref.shape[0]

    @pl.when(row == 0)
    def _():
        dk_s[...] = jnp.zeros_like(dk_s)
        dv_s[...] = jnp.zeros_like(dv_s)
        z_s[...] = jnp.zeros_like(z_s)

        @pl.loop(0, blocks)
        def _(b):
            kt_s[b] = kv_ref[b, :, :HD].astype(jnp.float32).T.astype(jnp.bfloat16)

    qs = [qd_ref[0, :, j * HD : (j + 1) * HD] for j in range(GRP)]
    gs = [qd_ref[0, :, (GRP + j) * HD : (GRP + j + 1) * HD] for j in range(GRP)]
    q_all = jnp.concatenate(qs, axis=0)
    g_all = jnp.concatenate(gs, axis=0)

    def dot(a, b):
        return jnp.dot(a, b, preferred_element_type=jnp.float32)

    def dot_nt(a, b):
        return lax.dot_general(a, b, NT, preferred_element_type=jnp.float32)

    def pair(c1, c2):
        k = jnp.concatenate([kv_ref[c1, :, :HD], kv_ref[c2, :, :HD]], axis=0)
        v = jnp.concatenate([kv_ref[c1, :, HD:], kv_ref[c2, :, HD:]], axis=0)
        return k, v

    diag = edge_ref[row, 0]
    first_bias = jnp.where(edge_ref[row, 1] > 0, NEG, 0.0).astype(jnp.float32)
    k0, v0 = pair(0, diag)
    s_all = dot_nt(k0, q_all) * (SCALE * LOG2E)
    dp_all = dot_nt(v0, g_all)
    key_pos = lax.broadcasted_iota(jnp.int32, (BLK, BLK), 0)
    query_pos = lax.broadcasted_iota(jnp.int32, (BLK, BLK), 1)
    causal = key_pos <= query_pos
    state = []
    for j in range(GRP):
        cut = slice(j * BLK, (j + 1) * BLK)
        s = jnp.concatenate(
            [s_all[:BLK, cut] + first_bias, jnp.where(causal, s_all[BLK:, cut], NEG)], axis=0
        )
        dp = dp_all[:, cut]
        m = jnp.max(s, axis=0, keepdims=True)
        e = jnp.exp2(s - m)
        e_s[0, j] = e
        dp_s[0, j] = dp
        m_s[0, j] = jnp.broadcast_to(m, (8, BLK))
        state += [m, jnp.sum(e, axis=0, keepdims=True), jnp.sum(e * dp, axis=0, keepdims=True)]

    def entry(t, j):
        slot = 2 * (t - 1)
        c1 = cols_ref[row, j * blocks + slot]
        c2 = cols_ref[row, j * blocks + slot + 1]
        return slot, c1, c2

    def forward(t, state):
        out = []
        for j in range(GRP):
            m, l, u = state[3 * j : 3 * j + 3]
            slot, c1, c2 = entry(t, j)
            n = cnt_ref[row, j]
            b1 = jnp.where(slot < n, 0.0, NEG).astype(jnp.float32)
            b2 = jnp.where(slot + 1 < n, 0.0, NEG).astype(jnp.float32)
            k, v = pair(c1, c2)
            s = dot_nt(k, qs[j]) * (SCALE * LOG2E)
            s = jnp.concatenate([s[:BLK] + b1, s[BLK:] + b2], axis=0)
            dp = dot_nt(v, gs[j])
            m_new = jnp.maximum(m, jnp.max(s, axis=0, keepdims=True))
            e = jnp.exp2(s - m_new)
            alpha = jnp.exp2(m - m_new)
            e_s[t, j] = e
            dp_s[t, j] = dp
            m_s[t, j] = jnp.broadcast_to(m_new, (8, BLK))
            out += [
                m_new,
                l * alpha + jnp.sum(e, axis=0, keepdims=True),
                u * alpha + jnp.sum(e * dp, axis=0, keepdims=True),
            ]
        return tuple(out)

    steps = steps_ref[row, 0]
    state = lax.fori_loop(1, steps, forward, tuple(state))

    top, inv, pull = [], [], []
    for j in range(GRP):
        m, l, u = state[3 * j : 3 * j + 3]
        inv_l = 1.0 / l
        log_norm = m * LN2 + jnp.log(l)
        top.append(m)
        inv.append(inv_l)
        pull.append((2.0 * ZLOSS) * log_norm - u * inv_l)
        z_s[j : j + 1, :] += log_norm * log_norm

    def weights(t, j):
        factor = jnp.exp2(m_s[t, j][:1] - top[j]) * inv[j]
        probs = e_s[t, j] * factor
        dscore = probs * (dp_s[t, j] + pull[j])
        return probs.astype(jnp.bfloat16), dscore.astype(jnp.bfloat16)

    first = [weights(0, j) for j in range(GRP)]
    p_all = jnp.concatenate([w[0] for w in first], axis=1)
    d_all = jnp.concatenate([w[1] for w in first], axis=1)
    dk = dot(d_all, q_all)
    dv = dot(p_all, g_all)
    dk_s[0] += dk[:BLK]
    dv_s[0] += dv[:BLK]
    dk_s[diag] += dk[BLK:]
    dv_s[diag] += dv[BLK:]
    kt = jnp.concatenate([kt_s[0], kt_s[diag]], axis=1)
    dqt = dot(kt, d_all)
    for j in range(GRP):
        dqt_s[j] = dqt[:, j * BLK : (j + 1) * BLK]

    @pl.loop(1, steps)
    def _(t):
        for j in range(GRP):
            _, c1, c2 = entry(t, j)
            p_low, d_low = weights(t, j)
            dk = dot(d_low, qs[j])
            dv = dot(p_low, gs[j])
            kt = jnp.concatenate([kt_s[c1], kt_s[c2]], axis=1)
            dqt_s[j] += dot(kt, d_low)
            dk_s[c1] += dk[:BLK]
            dv_s[c1] += dv[:BLK]
            dk_s[c2] += dk[BLK:]
            dv_s[c2] += dv[BLK:]

    for j in range(GRP):
        dq_ref[0, :, j * HD : (j + 1) * HD] = (dqt_s[j] * SCALE).T.astype(jnp.bfloat16)

    @pl.when(row == pl.num_programs(0) - 1)
    def _():
        dkv_ref[:, :, :HD] = (dk_s[...] * SCALE).astype(jnp.bfloat16)
        dkv_ref[:, :, HD:] = dv_s[...].astype(jnp.bfloat16)
        z_ref[...] = z_s[...]


def attention(qd, kv, cols, cnt, steps, edge):
    rows = qd.shape[0]
    blocks = kv.shape[0]
    max_steps = blocks // 2
    return pl.pallas_call(
        attention_body,
        out_shape=(
            jax.ShapeDtypeStruct((rows, BLK, GRP * HD), jnp.bfloat16),
            jax.ShapeDtypeStruct((blocks, BLK, 2 * HD), jnp.bfloat16),
            jax.ShapeDtypeStruct((8, BLK), jnp.float32),
        ),
        grid_spec=pltpu.PrefetchScalarGridSpec(
            num_scalar_prefetch=4,
            grid=(rows,),
            in_specs=[
                pl.BlockSpec((1, BLK, 2 * GRP * HD), lambda i, *_: (i, 0, 0)),
                pl.BlockSpec((blocks, BLK, 2 * HD), lambda i, *_: (0, 0, 0)),
            ],
            out_specs=[
                pl.BlockSpec((1, BLK, GRP * HD), lambda i, *_: (i, 0, 0)),
                pl.BlockSpec((blocks, BLK, 2 * HD), lambda i, *_: (0, 0, 0)),
                pl.BlockSpec((8, BLK), lambda i, *_: (0, 0)),
            ],
            scratch_shapes=[
                pltpu.VMEM((max_steps, GRP, 2 * BLK, BLK), jnp.float32),
                pltpu.VMEM((max_steps, GRP, 2 * BLK, BLK), jnp.float32),
                pltpu.VMEM((max_steps, GRP, 8, BLK), jnp.float32),
                pltpu.VMEM((blocks, BLK, HD), jnp.float32),
                pltpu.VMEM((blocks, BLK, HD), jnp.float32),
                pltpu.VMEM((blocks, HD, BLK), jnp.bfloat16),
                pltpu.VMEM((GRP, HD, BLK), jnp.float32),
                pltpu.VMEM((8, BLK), jnp.float32),
            ],
        ),
        compiler_params=pltpu.CompilerParams(
            dimension_semantics=("arbitrary",), vmem_limit_bytes=58 << 20
        ),
        cost_estimate=pl.CostEstimate(
            flops=40_000_000_000, transcendentals=4_000_000, bytes_accessed=9_000_000
        ),
        name="block_attention",
    )(cols, cnt, steps, edge, qd, kv)


def pack_body(a_ref, b_ref, out_ref, hold, in_sem, out_sem):
    heads = out_ref.shape[0]
    width = out_ref.shape[2] // 2
    loads = [
        [
            pltpu.make_async_copy(
                ref.at[0, :, pl.ds(u * width, width)],
                hold.at[u, :, pl.ds(n * width, width)],
                in_sem.at[n, u],
            )
            for n, ref in enumerate((a_ref, b_ref))
        ]
        for u in range(heads)
    ]
    stores = [pltpu.make_async_copy(hold.at[u], out_ref.at[u], out_sem.at[u]) for u in range(heads)]
    for both in loads:
        for copy in both:
            copy.start()
    for u in range(heads):
        for copy in loads[u]:
            copy.wait()
        stores[u].start()
    for copy in stores:
        copy.wait()


def pack(a, b):
    tok = a.shape[1]
    shape = (KVH, tok, 2 * a.shape[2] // KVH)
    return pl.pallas_call(
        pack_body,
        out_shape=jax.ShapeDtypeStruct(shape, a.dtype),
        in_specs=[pl.BlockSpec(memory_space=pl.ANY)] * 2,
        out_specs=pl.BlockSpec(memory_space=pl.ANY),
        scratch_shapes=[
            pltpu.VMEM(shape, a.dtype),
            pltpu.SemaphoreType.DMA((2, KVH)),
            pltpu.SemaphoreType.DMA((KVH,)),
        ],
        cost_estimate=pl.CostEstimate(flops=0, transcendentals=0, bytes_accessed=8 * a.size),
        name="pack",
    )(a, b)


def block_of(part, i):
    return (i // 2) * (2 * PARTS) + 2 * part + i % 2


def work_lists(mask, part):
    blocks = mask.shape[2]
    rows = blocks // PARTS
    mask = mask.reshape(GRP, rows // 2, PARTS, 2, blocks)
    mask = lax.dynamic_index_in_dim(mask, part, axis=2, keepdims=False).reshape(GRP, rows, blocks)
    mask = jnp.transpose(mask, (1, 0, 2))
    col = jnp.arange(blocks, dtype=jnp.int32)
    row = jnp.arange(rows, dtype=jnp.int32)
    own = block_of(part, row)
    other = (mask > 0) & (col > 0)[None, None, :] & (col[None, :] != own[:, None])[:, None, :]
    other = other.astype(jnp.int32)
    before = (col[None, :] < col[:, None]).astype(jnp.int32)
    rank = jnp.sum(other[:, :, None, :] * before[None, None], axis=3)
    place = (col // 2 % PARTS) * rows + col // (2 * PARTS) * 2 + col % 2
    hit = (rank[:, :, None, :] == col[None, None, :, None]) & (other[:, :, None, :] > 0)
    cols = jnp.sum(jnp.where(hit, place[None, None, None, :], 0), axis=3)
    cnt = jnp.sum(other, axis=2)
    steps = 1 + (jnp.max(cnt, axis=1) + 1) // 2
    edge = jnp.stack([part * rows + row, (own == 0).astype(jnp.int32)], axis=1)
    return cols.reshape(rows, GRP * blocks), cnt, steps[:, None], edge


def body(queries, keys, values, out_grad, block_mask):
    tok = queries.shape[1]
    dps = lax.axis_size("dp")
    blocks = block_mask.shape[1]
    me = lax.axis_index("ctx")

    def at(u, x):
        return (u // 2 * PARTS + x) * 2 + u % 2

    part = me // 2 % PARTS
    core = me % 2
    kv_head = me // (2 * PARTS) * 2 + core
    column = [[at(u, x) for u in range(KVH)] for x in range(PARTS)]
    ring = [[at(u, x) for x in range(PARTS)] for u in range(KVH)]
    wide = [[d * PARTS * KVH + at(u, x) for d in range(dps) for x in range(PARTS)] for u in range(KVH)]

    def exchange(a):
        return lax.all_to_all(a, "ctx", 0, 0, axis_index_groups=column, tiled=True)

    kv_part = exchange(pack(keys, values))
    qd_send = pack(queries, out_grad)
    kv_part, qd_send = lax.optimization_barrier((kv_part, qd_send))
    kv = lax.all_gather(kv_part, "ctx", axis=0, axis_index_groups=ring, tiled=True)
    qd = exchange(qd_send)

    mask = lax.dynamic_slice(block_mask, (kv_head * GRP, 0, 0), (GRP, blocks, blocks))
    cols, cnt, steps, edge = work_lists(mask, part)
    dq, dkv, z = attention(qd, kv, cols, cnt, steps, edge)

    dkv_part = lax.psum_scatter(dkv, "ctx", scatter_dimension=0, axis_index_groups=ring, tiled=True)
    query_grad = exchange(dq).transpose(1, 0, 2).reshape(1, tok, H * HD)

    half = jnp.arange(PARTS, dtype=jnp.int32)
    z_send = jnp.where(
        (half // 2 == core)[:, None, None], jnp.tile(z[:GRP].reshape(2, 2, BLK), (2, 1, 1)), 0.0
    )
    z_back = lax.all_to_all(
        jnp.tile(z_send, (dps, 1, 1)), ("dp", "ctx"), 0, 0, axis_index_groups=wide, tiled=True
    )
    z_two = jnp.sum(z_back, axis=(0, 2)) * (ZLOSS / (dps * blocks * BLK))
    z_mine = jnp.where(core == 0, z_two[0], z_two[1])
    z_mate = jnp.where(core == 0, z_two[1], z_two[0])
    swap = [(at(u - u % 2 + x // 2, x), at(u - u % 2 + 1 - x // 2, x)) for u in range(0, KVH, 2) for x in range(PARTS)]
    z_swap = lax.ppermute(z_mate, "ctx", swap)
    z_own = jnp.where(part // 2 == core, z_mine, z_swap)[None]

    dkv_back = exchange(dkv_part).transpose(1, 0, 2)
    key_grad = dkv_back[:, :, :HD].reshape(1, tok, KVH * HD)
    value_grad = dkv_back[:, :, HD:].reshape(1, tok, KVH * HD)
    return query_grad, key_grad, value_grad, z_own


def solution(mesh):
    return jax.shard_map(
        body,
        mesh=mesh,
        in_specs=(
            P("dp", "ctx", None),
            P("dp", "ctx", None),
            P("dp", "ctx", None),
            P("dp", "ctx", None),
            P(),
        ),
        out_specs=(P("dp", "ctx", None), P("dp", "ctx", None), P("dp", "ctx", None), P("ctx")),
        check_vma=False,
    )
```

```python
import math

import jax
import jax.numpy as jnp
from jax import lax
from jax.experimental import pallas as pl
from jax.experimental.pallas import tpu as pltpu
from jax.sharding import PartitionSpec as P

H = 32
KVH = 8
HD = 128
BLK = 128
PAIR = 2
ROWS = 2
Z_ROWS = 64

ZLOSS = 0.05
NEG = -1e30
LOG2E = 1.0 / math.log(2.0)
LN2 = math.log(2.0)
SCALE = HD ** (-0.5)

NT = (((1,), (1,)), ((), ()))


def attention_body(
    cols_ref, cnt_ref, steps_ref, edge_ref,
    qd_ref, own_ref, mate_ref,
    send_ref, give_ref, z_ref,
    kv_s, e_s, dp_s, m_s, dk_s, dv_s, kt_s, dqt_s, sem,
):
    step = pl.program_id(0)
    blocks = kv_s.shape[0]
    half = blocks // 2
    core = edge_ref[0, 2]

    @pl.when(step == 0)
    def _():
        own = pltpu.make_async_copy(
            own_ref.at[:, :, pl.ds(4 * HD, 2 * HD)], kv_s.at[pl.ds(core * half, half)], sem.at[0]
        )
        mate = pltpu.make_async_copy(mate_ref, kv_s.at[pl.ds((1 - core) * half, half)], sem.at[1])
        own.start()
        mate.start()
        dk_s[...] = jnp.zeros_like(dk_s)
        dv_s[...] = jnp.zeros_like(dv_s)
        z_ref[...] = jnp.zeros_like(z_ref)
        own.wait()
        mate.wait()

        @pl.loop(0, blocks // 4)
        def _(b):
            for n in range(4):
                kt_s[4 * b + n] = kv_s[4 * b + n, :, :HD].T

    lanes = [(s, j) for s in range(ROWS) for j in range(PAIR)]
    qs = [qd_ref[s, :, j * HD : (j + 1) * HD] for s, j in lanes]
    gs = [qd_ref[s, :, (PAIR + j) * HD : (PAIR + j + 1) * HD] for s, j in lanes]

    def dot(a, b):
        return jnp.dot(a, b, preferred_element_type=jnp.float32)

    def dot_nt(a, b):
        return lax.dot_general(a, b, NT, preferred_element_type=jnp.float32)

    def pair(c1, c2):
        k = jnp.concatenate([kv_s[c1, :, :HD], kv_s[c2, :, :HD]], axis=0)
        v = jnp.concatenate([kv_s[c1, :, HD:], kv_s[c2, :, HD:]], axis=0)
        return k, v

    key_pos = lax.broadcasted_iota(jnp.int32, (BLK, BLK), 0)
    query_pos = lax.broadcasted_iota(jnp.int32, (BLK, BLK), 1)
    causal = key_pos <= query_pos
    state, row_q, row_g, diags = [], [], [], []
    for s in range(ROWS):
        diag = core * half + ROWS * step + s
        diags.append(diag)
        row_q.append(jnp.concatenate(qs[s * PAIR : (s + 1) * PAIR], axis=0))
        row_g.append(jnp.concatenate(gs[s * PAIR : (s + 1) * PAIR], axis=0))
        k0, v0 = pair(0, diag)
        s_all = dot_nt(k0, row_q[s]) * (SCALE * LOG2E)
        dp_all = dot_nt(v0, row_g[s])
        bias = jnp.where(diag == 0, NEG, 0.0).astype(jnp.float32)
        for j in range(PAIR):
            cut = slice(j * BLK, (j + 1) * BLK)
            sc = jnp.concatenate(
                [s_all[:BLK, cut] + bias, jnp.where(causal, s_all[BLK:, cut], NEG)], axis=0
            )
            dp = dp_all[:, cut]
            m = jnp.max(sc, axis=0, keepdims=True)
            e = jnp.exp2(sc - m)
            n = s * PAIR + j
            e_s[0, n] = e
            dp_s[0, n] = dp
            m_s[0, n] = jnp.broadcast_to(m, (8, BLK))
            state += [m, jnp.sum(e, axis=0, keepdims=True), jnp.sum(e * dp, axis=0, keepdims=True)]

    def entry(t, n):
        slot = 2 * (t - 1)
        return slot, cols_ref[step, n * blocks + slot], cols_ref[step, n * blocks + slot + 1]

    def forward(t, state):
        out = []
        for n in range(len(lanes)):
            m, l, u = state[3 * n : 3 * n + 3]
            slot, c1, c2 = entry(t, n)
            count = cnt_ref[step, n]
            b1 = jnp.where(slot < count, 0.0, NEG).astype(jnp.float32)
            b2 = jnp.where(slot + 1 < count, 0.0, NEG).astype(jnp.float32)
            k, v = pair(c1, c2)
            sc = dot_nt(k, qs[n]) * (SCALE * LOG2E)
            sc = jnp.concatenate([sc[:BLK] + b1, sc[BLK:] + b2], axis=0)
            dp = dot_nt(v, gs[n])
            m_new = jnp.maximum(m, jnp.max(sc, axis=0, keepdims=True))
            e = jnp.exp2(sc - m_new)
            alpha = jnp.exp2(m - m_new)
            e_s[t, n] = e
            dp_s[t, n] = dp
            m_s[t, n] = jnp.broadcast_to(m_new, (8, BLK))
            out += [
                m_new,
                l * alpha + jnp.sum(e, axis=0, keepdims=True),
                u * alpha + jnp.sum(e * dp, axis=0, keepdims=True),
            ]
        return tuple(out)

    steps = steps_ref[step, 0]
    state = lax.fori_loop(1, steps, forward, tuple(state))

    top, inv, pull = [], [], []
    for n, (s, j) in enumerate(lanes):
        m, l, u = state[3 * n : 3 * n + 3]
        inv_l = 1.0 / l
        log_norm = m * LN2 + jnp.log(l)
        top.append(m)
        inv.append(inv_l)
        pull.append((2.0 * ZLOSS) * log_norm - u * inv_l)
        z_ref[j : j + 1, :] += log_norm * log_norm

    def weights(t, n):
        factor = jnp.exp2(m_s[t, n][:1] - top[n]) * inv[n]
        probs = e_s[t, n] * factor
        dscore = probs * (dp_s[t, n] + pull[n])
        return probs.astype(jnp.bfloat16), dscore.astype(jnp.bfloat16)

    dk0, dv0 = [], []
    for s in range(ROWS):
        first = [weights(0, s * PAIR + j) for j in range(PAIR)]
        p_all = jnp.concatenate([w[0] for w in first], axis=1)
        d_all = jnp.concatenate([w[1] for w in first], axis=1)
        dk = dot(d_all, row_q[s])
        dv = dot(p_all, row_g[s])
        dk0.append(dk[:BLK])
        dv0.append(dv[:BLK])
        dk_s[diags[s]] += dk[BLK:]
        dv_s[diags[s]] += dv[BLK:]
        dqt = dot(jnp.concatenate([kt_s[0], kt_s[diags[s]]], axis=1), d_all)
        for j in range(PAIR):
            dqt_s[s * PAIR + j] = dqt[:, j * BLK : (j + 1) * BLK]
    dk_s[0] += sum(dk0[1:], dk0[0])
    dv_s[0] += sum(dv0[1:], dv0[0])

    @pl.loop(1, steps)
    def _(t):
        for n in range(len(lanes)):
            _, c1, c2 = entry(t, n)
            p_low, d_low = weights(t, n)
            dk = dot(d_low, qs[n])
            dv = dot(p_low, gs[n])
            dqt_s[n] += dot(jnp.concatenate([kt_s[c1], kt_s[c2]], axis=1), d_low)
            dk_s[c1] += dk[:BLK]
            dv_s[c1] += dv[:BLK]
            dk_s[c2] += dk[BLK:]
            dv_s[c2] += dv[BLK:]

    for n, (s, j) in enumerate(lanes):
        send_ref[ROWS * step + s, :, j * HD : (j + 1) * HD] = (dqt_s[n] * SCALE).T.astype(jnp.bfloat16)

    @pl.when(step == pl.num_programs(0) - 1)
    def _():
        @pl.loop(0, half)
        def _(i):
            mine = core * half + i
            other = (1 - core) * half + i
            send_ref[i, :, 2 * HD : 3 * HD] = (dk_s[mine] * SCALE).astype(jnp.bfloat16)
            send_ref[i, :, 3 * HD :] = dv_s[mine].astype(jnp.bfloat16)
            give_ref[i, :, :HD] = (dk_s[other] * SCALE).astype(jnp.bfloat16)
            give_ref[i, :, HD:] = dv_s[other].astype(jnp.bfloat16)


def attention(recv, mate, cols, cnt, steps, edge):
    half = recv.shape[0]
    blocks = 2 * half
    lanes = ROWS * PAIR
    max_steps = half
    return pl.pallas_call(
        attention_body,
        out_shape=(
            jax.ShapeDtypeStruct((half, BLK, 4 * HD), jnp.bfloat16),
            jax.ShapeDtypeStruct((half, BLK, 2 * HD), jnp.bfloat16),
            jax.ShapeDtypeStruct((Z_ROWS, BLK), jnp.float32),
        ),
        grid_spec=pltpu.PrefetchScalarGridSpec(
            num_scalar_prefetch=4,
            grid=(half // ROWS,),
            in_specs=[
                pl.BlockSpec((ROWS, BLK, 4 * HD), lambda i, *_: (i, 0, 0)),
                pl.BlockSpec(memory_space=pl.ANY),
                pl.BlockSpec(memory_space=pl.ANY),
            ],
            out_specs=[
                pl.BlockSpec((half, BLK, 4 * HD), lambda i, *_: (0, 0, 0)),
                pl.BlockSpec((half, BLK, 2 * HD), lambda i, *_: (0, 0, 0)),
                pl.BlockSpec((Z_ROWS, BLK), lambda i, *_: (0, 0)),
            ],
            scratch_shapes=[
                pltpu.VMEM((blocks, BLK, 2 * HD), jnp.bfloat16),
                pltpu.VMEM((max_steps, lanes, 2 * BLK, BLK), jnp.float32),
                pltpu.VMEM((max_steps, lanes, 2 * BLK, BLK), jnp.float32),
                pltpu.VMEM((max_steps, lanes, 8, BLK), jnp.float32),
                pltpu.VMEM((blocks, BLK, HD), jnp.float32),
                pltpu.VMEM((blocks, BLK, HD), jnp.float32),
                pltpu.VMEM((blocks, HD, BLK), jnp.bfloat16),
                pltpu.VMEM((lanes, HD, BLK), jnp.float32),
                pltpu.SemaphoreType.DMA((2,)),
            ],
        ),
        compiler_params=pltpu.CompilerParams(
            dimension_semantics=("arbitrary",), vmem_limit_bytes=58 << 20
        ),
        cost_estimate=pl.CostEstimate(
            flops=40_000_000_000, transcendentals=4_000_000, bytes_accessed=9_000_000
        ),
        name="block_attention",
    )(cols, cnt, steps, edge, recv, recv, mate)


def pack_body(q_ref, g_ref, k_ref, v_ref, out_ref, hold, in_sem, out_sem):
    chips = out_ref.shape[0]

    def load(p, n):
        ref, width, start, place = (
            (q_ref, 2 * HD, 2 * HD * p, 0),
            (g_ref, 2 * HD, 2 * HD * p, 2 * HD),
            (k_ref, HD, HD * (p // 2), 4 * HD),
            (v_ref, HD, HD * (p // 2), 5 * HD),
        )[n]
        return pltpu.make_async_copy(
            ref.at[0, :, pl.ds(start, width)], hold.at[p, :, pl.ds(place, width)], in_sem.at[p, n]
        )

    loads = [[load(p, n) for n in range(4)] for p in range(chips)]
    stores = [pltpu.make_async_copy(hold.at[p], out_ref.at[p], out_sem.at[p]) for p in range(chips)]
    for four in loads:
        for copy in four:
            copy.start()
    for p in range(chips):
        for copy in loads[p]:
            copy.wait()
        stores[p].start()
    for copy in stores:
        copy.wait()


def pack(queries, out_grad, keys, values):
    tok = queries.shape[1]
    chips = H // PAIR
    shape = (chips, tok, 6 * HD)
    return pl.pallas_call(
        pack_body,
        out_shape=jax.ShapeDtypeStruct(shape, queries.dtype),
        in_specs=[pl.BlockSpec(memory_space=pl.ANY)] * 4,
        out_specs=pl.BlockSpec(memory_space=pl.ANY),
        scratch_shapes=[
            pltpu.VMEM(shape, queries.dtype),
            pltpu.SemaphoreType.DMA((chips, 4)),
            pltpu.SemaphoreType.DMA((chips,)),
        ],
        name="pack",
    )(queries, out_grad, keys, values)


def merge_body(send_ref, got_ref, out_ref):
    out_ref[...] = (send_ref[...].astype(jnp.float32) + got_ref[...].astype(jnp.float32)).astype(out_ref.dtype)


def merge(send, got):
    part = send.shape[0] // 4
    lower = pl.BlockSpec((part, BLK, 2 * HD), lambda i: (i, 0, 1))
    return pl.pallas_call(
        merge_body,
        out_shape=jax.ShapeDtypeStruct(send.shape, send.dtype),
        grid=(4,),
        in_specs=[lower, pl.BlockSpec((part, BLK, 2 * HD), lambda i: (i, 0, 0))],
        out_specs=lower,
        input_output_aliases={0: 0},
        name="merge",
    )(send, got)


def unpack_body(back_ref, dq_ref, dk_ref, dv_ref):
    for n in range(back_ref.shape[0]):
        dq_ref[0, :, n * 2 * HD : (n + 1) * 2 * HD] = back_ref[n, :, : 2 * HD]
    for g in range(back_ref.shape[0] // 2):
        both = back_ref[2 * g, :, 2 * HD :].astype(jnp.float32) + back_ref[2 * g + 1, :, 2 * HD :].astype(jnp.float32)
        dk_ref[0, :, g * HD : (g + 1) * HD] = both[:, :HD].astype(dk_ref.dtype)
        dv_ref[0, :, g * HD : (g + 1) * HD] = both[:, HD:].astype(dv_ref.dtype)


def unpack(back):
    chips, tok = back.shape[:2]
    cut = 4
    return pl.pallas_call(
        unpack_body,
        out_shape=(
            jax.ShapeDtypeStruct((1, tok, H * HD), back.dtype),
            jax.ShapeDtypeStruct((1, tok, KVH * HD), back.dtype),
            jax.ShapeDtypeStruct((1, tok, KVH * HD), back.dtype),
        ),
        grid=(cut,),
        in_specs=[pl.BlockSpec((chips // cut, tok, 4 * HD), lambda i: (i, 0, 0))],
        out_specs=[
            pl.BlockSpec((1, tok, H * HD // cut), lambda i: (0, 0, i)),
            pl.BlockSpec((1, tok, KVH * HD // cut), lambda i: (0, 0, i)),
            pl.BlockSpec((1, tok, KVH * HD // cut), lambda i: (0, 0, i)),
        ],
        name="unpack",
    )(back)


def work_lists(mask, core):
    blocks = mask.shape[2]
    half = blocks // 2
    mask = lax.dynamic_index_in_dim(mask.reshape(PAIR, half, 2, blocks), core, axis=2, keepdims=False)
    mask = jnp.transpose(mask.reshape(PAIR, half // ROWS, ROWS, blocks), (1, 2, 0, 3))
    col = jnp.arange(blocks, dtype=jnp.int32)
    own = (2 * jnp.arange(half, dtype=jnp.int32) + core).reshape(half // ROWS, ROWS)
    other = (mask > 0) & (col > 0) & (col != own[:, :, None, None])
    other = other.astype(jnp.int32).reshape(half // ROWS, ROWS * PAIR, blocks)
    before = (col[None, :] < col[:, None]).astype(jnp.int32)
    rank = jnp.sum(other[:, :, None, :] * before[None, None], axis=3)
    place = col % 2 * half + col // 2
    hit = (rank[:, :, None, :] == col[None, None, :, None]) & (other[:, :, None, :] > 0)
    cols = jnp.sum(jnp.where(hit, place[None, None, None, :], 0), axis=3)
    cnt = jnp.sum(other, axis=2)
    steps = 1 + (jnp.max(cnt, axis=1) + 1) // 2
    edge = jnp.full((1, 3), core, jnp.int32)
    return cols.reshape(half // ROWS, ROWS * PAIR * blocks), cnt, steps[:, None], edge


def body(queries, keys, values, out_grad, block_mask):
    dps = lax.axis_size("dp")
    ctx = lax.axis_size("ctx")
    blocks = block_mask.shape[1]
    me = lax.axis_index("ctx")
    chip, core = me // 2, me % 2
    same = [[2 * p + c for p in range(ctx // 2)] for c in range(2)]
    mates = [(i, i ^ 1) for i in range(ctx)]
    wide = [[d * ctx + 2 * p + c for d in range(dps) for c in range(2)] for p in range(ctx // 2)]

    def exchange(a):
        return lax.all_to_all(a, "ctx", 0, 0, axis_index_groups=same, tiled=True)

    recv = exchange(pack(queries, out_grad, keys, values))
    mate = lax.ppermute(recv[:, :, 4 * HD :], "ctx", mates)

    mask = lax.dynamic_slice(block_mask, (chip * PAIR, 0, 0), (PAIR, blocks, blocks))
    send, give, z = attention(recv, mate, *work_lists(mask, core))

    z_all = lax.all_gather(z, ("dp", "ctx"), axis_index_groups=wide)
    send = merge(send, lax.ppermute(give, "ctx", mates))
    query_grad, key_grad, value_grad = unpack(exchange(send))
    z_two = jnp.sum(z_all[:, :PAIR], axis=(0, 2)) * (ZLOSS / (dps * blocks * BLK))
    z_own = jnp.where(core == 0, z_two[0], z_two[1])[None]
    return query_grad, key_grad, value_grad, z_own


def solution(mesh):
    return jax.shard_map(
        body,
        mesh=mesh,
        in_specs=(
            P("dp", "ctx", None),
            P("dp", "ctx", None),
            P("dp", "ctx", None),
            P("dp", "ctx", None),
            P(),
        ),
        out_specs=(P("dp", "ctx", None), P("dp", "ctx", None), P("dp", "ctx", None), P("ctx")),
        check_vma=False,
    )
```

```python
import math

import jax
import jax.numpy as jnp
from jax import lax
from jax.experimental import pallas as pl
from jax.experimental.pallas import tpu as pltpu
from jax.sharding import PartitionSpec as P

H = 32
KVH = 8
HD = 128
BLK = 128
PAIR = 2
ROWS = 2
Z_ROWS = 8

ZLOSS = 0.05
NEG = -1e30
LOG2E = 1.0 / math.log(2.0)
LN2 = math.log(2.0)
SCALE = HD ** (-0.5)

NT = (((1,), (1,)), ((), ()))


def attention_body(
    cols_ref, cnt_ref, steps_ref, edge_ref,
    qd_ref, own_ref, mate_ref,
    send_ref, give_ref, z_ref,
    kv_s, e_s, dp_s, m_s, dk_s, dv_s, kt_s, dqt_s, sem,
):
    step = pl.program_id(0)
    blocks = kv_s.shape[0]
    half = blocks // 2
    core = edge_ref[0, 2]

    @pl.when(step == 0)
    def _():
        own = pltpu.make_async_copy(
            own_ref.at[:, :, pl.ds(4 * HD, 2 * HD)], kv_s.at[pl.ds(core * half, half)], sem.at[0]
        )
        mate = pltpu.make_async_copy(mate_ref, kv_s.at[pl.ds((1 - core) * half, half)], sem.at[1])
        own.start()
        mate.start()
        dk_s[...] = jnp.zeros_like(dk_s)
        dv_s[...] = jnp.zeros_like(dv_s)
        z_ref[...] = jnp.zeros_like(z_ref)
        own.wait()
        mate.wait()

        @pl.loop(0, blocks // 4)
        def _(b):
            for n in range(4):
                kt_s[4 * b + n] = kv_s[4 * b + n, :, :HD].T

    lanes = [(s, j) for s in range(ROWS) for j in range(PAIR)]
    qs = [qd_ref[s, :, j * HD : (j + 1) * HD] for s, j in lanes]
    gs = [qd_ref[s, :, (PAIR + j) * HD : (PAIR + j + 1) * HD] for s, j in lanes]

    def dot(a, b):
        return jnp.dot(a, b, preferred_element_type=jnp.float32)

    def dot_nt(a, b):
        return lax.dot_general(a, b, NT, preferred_element_type=jnp.float32)

    def pair(c1, c2):
        k = jnp.concatenate([kv_s[c1, :, :HD], kv_s[c2, :, :HD]], axis=0)
        v = jnp.concatenate([kv_s[c1, :, HD:], kv_s[c2, :, HD:]], axis=0)
        return k, v

    key_pos = lax.broadcasted_iota(jnp.int32, (BLK, BLK), 0)
    query_pos = lax.broadcasted_iota(jnp.int32, (BLK, BLK), 1)
    causal = key_pos <= query_pos
    state, row_q, row_g, diags = [], [], [], []
    for s in range(ROWS):
        diag = core * half + ROWS * step + s
        diags.append(diag)
        row_q.append(jnp.concatenate(qs[s * PAIR : (s + 1) * PAIR], axis=0))
        row_g.append(jnp.concatenate(gs[s * PAIR : (s + 1) * PAIR], axis=0))
        k0, v0 = pair(0, diag)
        s_all = dot_nt(k0, row_q[s]) * (SCALE * LOG2E)
        dp_all = dot_nt(v0, row_g[s])
        bias = jnp.where(diag == 0, NEG, 0.0).astype(jnp.float32)
        for j in range(PAIR):
            cut = slice(j * BLK, (j + 1) * BLK)
            sc = jnp.concatenate(
                [s_all[:BLK, cut] + bias, jnp.where(causal, s_all[BLK:, cut], NEG)], axis=0
            )
            dp = dp_all[:, cut]
            m = jnp.max(sc, axis=0, keepdims=True)
            e = jnp.exp2(sc - m)
            n = s * PAIR + j
            e_s[0, n] = e
            dp_s[0, n] = dp
            m_s[0, n] = jnp.broadcast_to(m, (8, BLK))
            state += [m, jnp.sum(e, axis=0, keepdims=True), jnp.sum(e * dp, axis=0, keepdims=True)]

    def entry(t, n):
        slot = 2 * (t - 1)
        return slot, cols_ref[step, n * blocks + slot], cols_ref[step, n * blocks + slot + 1]

    def forward(t, state):
        out = []
        for n in range(len(lanes)):
            m, l, u = state[3 * n : 3 * n + 3]
            slot, c1, c2 = entry(t, n)
            count = cnt_ref[step, n]
            b1 = jnp.where(slot < count, 0.0, NEG).astype(jnp.float32)
            b2 = jnp.where(slot + 1 < count, 0.0, NEG).astype(jnp.float32)
            k, v = pair(c1, c2)
            sc = dot_nt(k, qs[n]) * (SCALE * LOG2E)
            sc = jnp.concatenate([sc[:BLK] + b1, sc[BLK:] + b2], axis=0)
            dp = dot_nt(v, gs[n])
            m_new = jnp.maximum(m, jnp.max(sc, axis=0, keepdims=True))
            e = jnp.exp2(sc - m_new)
            alpha = jnp.exp2(m - m_new)
            e_s[t, n] = e
            dp_s[t, n] = dp
            m_s[t, n] = jnp.broadcast_to(m_new, (8, BLK))
            out += [
                m_new,
                l * alpha + jnp.sum(e, axis=0, keepdims=True),
                u * alpha + jnp.sum(e * dp, axis=0, keepdims=True),
            ]
        return tuple(out)

    steps = steps_ref[step, 0]
    state = lax.fori_loop(1, steps, forward, tuple(state))

    top, inv, pull = [], [], []
    for n, (s, j) in enumerate(lanes):
        m, l, u = state[3 * n : 3 * n + 3]
        inv_l = 1.0 / l
        log_norm = m * LN2 + jnp.log(l)
        top.append(m)
        inv.append(inv_l)
        pull.append((2.0 * ZLOSS) * log_norm - u * inv_l)
        z_ref[j : j + 1, :] += log_norm * log_norm

    def weights(t, n):
        factor = jnp.exp2(m_s[t, n][:1] - top[n]) * inv[n]
        probs = e_s[t, n] * factor
        dscore = probs * (dp_s[t, n] + pull[n])
        return probs.astype(jnp.bfloat16), dscore.astype(jnp.bfloat16)

    dk0, dv0 = [], []
    for s in range(ROWS):
        first = [weights(0, s * PAIR + j) for j in range(PAIR)]
        p_all = jnp.concatenate([w[0] for w in first], axis=1)
        d_all = jnp.concatenate([w[1] for w in first], axis=1)
        dk = dot(d_all, row_q[s])
        dv = dot(p_all, row_g[s])
        dk0.append(dk[:BLK])
        dv0.append(dv[:BLK])
        dk_s[diags[s]] += dk[BLK:]
        dv_s[diags[s]] += dv[BLK:]
        dqt = dot(jnp.concatenate([kt_s[0], kt_s[diags[s]]], axis=1), d_all)
        for j in range(PAIR):
            dqt_s[s * PAIR + j] = dqt[:, j * BLK : (j + 1) * BLK]
    dk_s[0] += sum(dk0[1:], dk0[0])
    dv_s[0] += sum(dv0[1:], dv0[0])

    @pl.loop(1, steps)
    def _(t):
        for n in range(len(lanes)):
            _, c1, c2 = entry(t, n)
            p_low, d_low = weights(t, n)
            dk = dot(d_low, qs[n])
            dv = dot(p_low, gs[n])
            dqt_s[n] += dot(jnp.concatenate([kt_s[c1], kt_s[c2]], axis=1), d_low)
            dk_s[c1] += dk[:BLK]
            dv_s[c1] += dv[:BLK]
            dk_s[c2] += dk[BLK:]
            dv_s[c2] += dv[BLK:]

    for n, (s, j) in enumerate(lanes):
        send_ref[ROWS * step + s, :, j * HD : (j + 1) * HD] = (dqt_s[n] * SCALE).T.astype(jnp.bfloat16)

    @pl.when(step == pl.num_programs(0) - 1)
    def _():
        @pl.loop(0, half)
        def _(i):
            mine = core * half + i
            other = (1 - core) * half + i
            send_ref[i, :, 2 * HD : 3 * HD] = (dk_s[mine] * SCALE).astype(jnp.bfloat16)
            send_ref[i, :, 3 * HD :] = dv_s[mine].astype(jnp.bfloat16)
            give_ref[i, :, :HD] = (dk_s[other] * SCALE).astype(jnp.bfloat16)
            give_ref[i, :, HD:] = dv_s[other].astype(jnp.bfloat16)


def attention(recv, mate, cols, cnt, steps, edge):
    half = recv.shape[0]
    blocks = 2 * half
    lanes = ROWS * PAIR
    max_steps = half
    return pl.pallas_call(
        attention_body,
        out_shape=(
            jax.ShapeDtypeStruct((half, BLK, 4 * HD), jnp.bfloat16),
            jax.ShapeDtypeStruct((half, BLK, 2 * HD), jnp.bfloat16),
            jax.ShapeDtypeStruct((Z_ROWS, BLK), jnp.float32),
        ),
        grid_spec=pltpu.PrefetchScalarGridSpec(
            num_scalar_prefetch=4,
            grid=(half // ROWS,),
            in_specs=[
                pl.BlockSpec((ROWS, BLK, 4 * HD), lambda i, *_: (i, 0, 0)),
                pl.BlockSpec(memory_space=pl.ANY),
                pl.BlockSpec(memory_space=pl.ANY),
            ],
            out_specs=[
                pl.BlockSpec((half, BLK, 4 * HD), lambda i, *_: (0, 0, 0)),
                pl.BlockSpec((half, BLK, 2 * HD), lambda i, *_: (0, 0, 0)),
                pl.BlockSpec((Z_ROWS, BLK), lambda i, *_: (0, 0)),
            ],
            scratch_shapes=[
                pltpu.VMEM((blocks, BLK, 2 * HD), jnp.bfloat16),
                pltpu.VMEM((max_steps, lanes, 2 * BLK, BLK), jnp.float32),
                pltpu.VMEM((max_steps, lanes, 2 * BLK, BLK), jnp.float32),
                pltpu.VMEM((max_steps, lanes, 8, BLK), jnp.float32),
                pltpu.VMEM((blocks, BLK, HD), jnp.float32),
                pltpu.VMEM((blocks, BLK, HD), jnp.float32),
                pltpu.VMEM((blocks, HD, BLK), jnp.bfloat16),
                pltpu.VMEM((lanes, HD, BLK), jnp.float32),
                pltpu.SemaphoreType.DMA((2,)),
            ],
        ),
        compiler_params=pltpu.CompilerParams(
            dimension_semantics=("arbitrary",), vmem_limit_bytes=58 << 20
        ),
        cost_estimate=pl.CostEstimate(
            flops=40_000_000_000, transcendentals=4_000_000, bytes_accessed=9_000_000
        ),
        name="block_attention",
    )(cols, cnt, steps, edge, recv, recv, mate)


def pack_body(q_ref, g_ref, k_ref, v_ref, out_ref, hold, in_sem, out_sem):
    chips = out_ref.shape[0]

    def load(p, n):
        ref, width, start, place = (
            (q_ref, 2 * HD, 2 * HD * p, 0),
            (g_ref, 2 * HD, 2 * HD * p, 2 * HD),
            (k_ref, HD, HD * (p // 2), 4 * HD),
            (v_ref, HD, HD * (p // 2), 5 * HD),
        )[n]
        return pltpu.make_async_copy(
            ref.at[0, :, pl.ds(start, width)], hold.at[p, :, pl.ds(place, width)], in_sem.at[p, n]
        )

    loads = [[load(p, n) for n in range(4)] for p in range(chips)]
    stores = [pltpu.make_async_copy(hold.at[p], out_ref.at[p], out_sem.at[p]) for p in range(chips)]
    for four in loads:
        for copy in four:
            copy.start()
    for p in range(chips):
        for copy in loads[p]:
            copy.wait()
        stores[p].start()
    for copy in stores:
        copy.wait()


def pack(queries, out_grad, keys, values):
    tok = queries.shape[1]
    chips = H // PAIR
    shape = (chips, tok, 6 * HD)
    return pl.pallas_call(
        pack_body,
        out_shape=jax.ShapeDtypeStruct(shape, queries.dtype),
        in_specs=[pl.BlockSpec(memory_space=pl.ANY)] * 4,
        out_specs=pl.BlockSpec(memory_space=pl.ANY),
        scratch_shapes=[
            pltpu.VMEM(shape, queries.dtype),
            pltpu.SemaphoreType.DMA((chips, 4)),
            pltpu.SemaphoreType.DMA((chips,)),
        ],
        name="pack",
    )(queries, out_grad, keys, values)


def merge_body(send_ref, got_ref, out_ref, own_s, in_sem, out_sem):
    parts = in_sem.shape[0]
    part = own_s.shape[0] // parts

    def cut(n):
        return pl.ds(n * part, part)

    loads = [
        pltpu.make_async_copy(send_ref.at[cut(n), :, pl.ds(2 * HD, 2 * HD)], own_s.at[cut(n)], in_sem.at[n])
        for n in range(parts)
    ]
    stores = [
        pltpu.make_async_copy(own_s.at[cut(n)], out_ref.at[cut(n), :, pl.ds(2 * HD, 2 * HD)], out_sem.at[n])
        for n in range(parts)
    ]
    for copy in loads:
        copy.start()
    for n in range(parts):
        loads[n].wait()
        rows = slice(n * part, (n + 1) * part)
        both = own_s[rows].astype(jnp.float32) + got_ref[rows].astype(jnp.float32)
        own_s[rows] = both.astype(own_s.dtype)
        stores[n].start()
    for copy in stores:
        copy.wait()


def merge(send, got):
    return pl.pallas_call(
        merge_body,
        out_shape=jax.ShapeDtypeStruct(send.shape, send.dtype),
        in_specs=[pl.BlockSpec(memory_space=pl.ANY), pl.BlockSpec(memory_space=pltpu.VMEM)],
        out_specs=pl.BlockSpec(memory_space=pl.ANY),
        scratch_shapes=[
            pltpu.VMEM(got.shape, got.dtype),
            pltpu.SemaphoreType.DMA((4,)),
            pltpu.SemaphoreType.DMA((4,)),
        ],
        input_output_aliases={0: 0},
        compiler_params=pltpu.CompilerParams(vmem_limit_bytes=16 << 20),
        name="merge",
    )(send, got)


def unpack_body(back_ref, dq_ref, dk_ref, dv_ref, dk_s, dv_s, dq_sem, kv_sem):
    chips = back_ref.shape[0]
    copies = [
        pltpu.make_async_copy(
            back_ref.at[p, :, pl.ds(0, 2 * HD)], dq_ref.at[0, :, pl.ds(p * 2 * HD, 2 * HD)], dq_sem.at[p]
        )
        for p in range(chips)
    ]
    for copy in copies:
        copy.start()
    for g in range(chips // 2):
        both = back_ref[2 * g, :, 2 * HD :].astype(jnp.float32) + back_ref[2 * g + 1, :, 2 * HD :].astype(jnp.float32)
        dk_s[:, g * HD : (g + 1) * HD] = both[:, :HD].astype(dk_s.dtype)
        dv_s[:, g * HD : (g + 1) * HD] = both[:, HD:].astype(dv_s.dtype)
    copies += [
        pltpu.make_async_copy(dk_s, dk_ref.at[0], kv_sem.at[0]),
        pltpu.make_async_copy(dv_s, dv_ref.at[0], kv_sem.at[1]),
    ]
    for copy in copies[chips:]:
        copy.start()
    for copy in copies:
        copy.wait()


def unpack(back):
    chips, tok = back.shape[:2]
    return pl.pallas_call(
        unpack_body,
        out_shape=(
            jax.ShapeDtypeStruct((1, tok, H * HD), back.dtype),
            jax.ShapeDtypeStruct((1, tok, KVH * HD), back.dtype),
            jax.ShapeDtypeStruct((1, tok, KVH * HD), back.dtype),
        ),
        in_specs=[pl.BlockSpec(memory_space=pltpu.VMEM)],
        out_specs=[pl.BlockSpec(memory_space=pl.ANY)] * 3,
        scratch_shapes=[
            pltpu.VMEM((tok, KVH * HD), back.dtype),
            pltpu.VMEM((tok, KVH * HD), back.dtype),
            pltpu.SemaphoreType.DMA((chips,)),
            pltpu.SemaphoreType.DMA((2,)),
        ],
        compiler_params=pltpu.CompilerParams(vmem_limit_bytes=16 << 20),
        name="unpack",
    )(back)


def work_lists(mask, core):
    blocks = mask.shape[2]
    half = blocks // 2
    mask = lax.dynamic_index_in_dim(mask.reshape(PAIR, half, 2, blocks), core, axis=2, keepdims=False)
    mask = jnp.transpose(mask.reshape(PAIR, half // ROWS, ROWS, blocks), (1, 2, 0, 3))
    col = jnp.arange(blocks, dtype=jnp.int32)
    own = (2 * jnp.arange(half, dtype=jnp.int32) + core).reshape(half // ROWS, ROWS)
    other = (mask > 0) & (col > 0) & (col != own[:, :, None, None])
    other = other.astype(jnp.int32).reshape(half // ROWS, ROWS * PAIR, blocks)
    before = (col[None, :] < col[:, None]).astype(jnp.int32)
    rank = jnp.sum(other[:, :, None, :] * before[None, None], axis=3)
    place = col % 2 * half + col // 2
    hit = (rank[:, :, None, :] == col[None, None, :, None]) & (other[:, :, None, :] > 0)
    cols = jnp.sum(jnp.where(hit, place[None, None, None, :], 0), axis=3)
    cnt = jnp.sum(other, axis=2)
    steps = 1 + (jnp.max(cnt, axis=1) + 1) // 2
    edge = jnp.full((1, 3), core, jnp.int32)
    return cols.reshape(half // ROWS, ROWS * PAIR * blocks), cnt, steps[:, None], edge


def body(queries, keys, values, out_grad, block_mask):
    dps = lax.axis_size("dp")
    ctx = lax.axis_size("ctx")
    blocks = block_mask.shape[1]
    me = lax.axis_index("ctx")
    chip, core = me // 2, me % 2
    same = [[2 * p + c for p in range(ctx // 2)] for c in range(2)]
    mates = [(i, i ^ 1) for i in range(ctx)]

    def exchange(a):
        return lax.all_to_all(a, "ctx", 0, 0, axis_index_groups=same, tiled=True)

    recv = exchange(pack(queries, out_grad, keys, values))
    mate = lax.ppermute(recv[:, :, 4 * HD :], "ctx", mates)

    mask = lax.dynamic_slice(block_mask, (chip * PAIR, 0, 0), (PAIR, blocks, blocks))
    send, give, z = attention(recv, mate, *work_lists(mask, core))

    send = merge(send, lax.ppermute(give, "ctx", mates))
    send, z = lax.optimization_barrier((send, z))
    back = exchange(send)
    z_two = jnp.sum(lax.all_gather(z, "dp"), axis=(0, 2))[:PAIR] * (ZLOSS / (dps * blocks * BLK))
    z_mine = jnp.where(core == 0, z_two[0], z_two[1])
    z_mate = jnp.where(core == 0, z_two[1], z_two[0])
    z_own = (z_mine + lax.ppermute(z_mate, "ctx", mates))[None]
    query_grad, key_grad, value_grad = unpack(back)
    return query_grad, key_grad, value_grad, z_own


def solution(mesh):
    return jax.shard_map(
        body,
        mesh=mesh,
        in_specs=(
            P("dp", "ctx", None),
            P("dp", "ctx", None),
            P("dp", "ctx", None),
            P("dp", "ctx", None),
            P(),
        ),
        out_specs=(P("dp", "ctx", None), P("dp", "ctx", None), P("dp", "ctx", None), P("ctx")),
        check_vma=False,
    )
```

```python
import math

import jax
import jax.numpy as jnp
from jax import lax
from jax.experimental import pallas as pl
from jax.experimental.pallas import tpu as pltpu
from jax.sharding import PartitionSpec as P

H = 32
KVH = 8
HD = 128
BLK = 128
PAIR = 2
ROWS = 4
Z_ROWS = 8

ZLOSS = 0.05
NEG = -1e30
LOG2E = 1.0 / math.log(2.0)
LN2 = math.log(2.0)
SCALE = HD ** (-0.5)

NT = (((1,), (1,)), ((), ()))


def attention_body(
    cols_ref, cnt_ref, steps_ref, edge_ref,
    qd_ref, own_ref, mate_ref,
    send_ref, give_ref, z_ref,
    kv_s, e_s, dp_s, m_s, dk_s, dv_s, kt_s, dqt_s, sem,
):
    step = pl.program_id(0)
    blocks = kv_s.shape[0]
    half = blocks // 2
    core = edge_ref[0, 2]

    @pl.when(step == 0)
    def _():
        own = pltpu.make_async_copy(
            own_ref.at[:, :, pl.ds(4 * HD, 2 * HD)], kv_s.at[pl.ds(core * half, half)], sem.at[0]
        )
        mate = pltpu.make_async_copy(mate_ref, kv_s.at[pl.ds((1 - core) * half, half)], sem.at[1])
        own.start()
        mate.start()
        dk_s[...] = jnp.zeros_like(dk_s)
        dv_s[...] = jnp.zeros_like(dv_s)
        z_ref[...] = jnp.zeros_like(z_ref)
        own.wait()
        mate.wait()

        @pl.loop(0, blocks // 4)
        def _(b):
            for n in range(4):
                kt_s[4 * b + n] = kv_s[4 * b + n, :, :HD].T

    lanes = [(s, j) for s in range(ROWS) for j in range(PAIR)]
    qs = [qd_ref[s, :, j * HD : (j + 1) * HD] for s, j in lanes]
    gs = [qd_ref[s, :, (PAIR + j) * HD : (PAIR + j + 1) * HD] for s, j in lanes]

    def dot(a, b):
        return jnp.dot(a, b, preferred_element_type=jnp.float32)

    def dot_nt(a, b):
        return lax.dot_general(a, b, NT, preferred_element_type=jnp.float32)

    def pair(c1, c2):
        k = jnp.concatenate([kv_s[c1, :, :HD], kv_s[c2, :, :HD]], axis=0)
        v = jnp.concatenate([kv_s[c1, :, HD:], kv_s[c2, :, HD:]], axis=0)
        return k, v

    key_pos = lax.broadcasted_iota(jnp.int32, (BLK, BLK), 0)
    query_pos = lax.broadcasted_iota(jnp.int32, (BLK, BLK), 1)
    causal = key_pos <= query_pos
    state, row_q, row_g, diags = [], [], [], []
    for s in range(ROWS):
        diag = core * half + ROWS * step + s
        diags.append(diag)
        row_q.append(jnp.concatenate(qs[s * PAIR : (s + 1) * PAIR], axis=0))
        row_g.append(jnp.concatenate(gs[s * PAIR : (s + 1) * PAIR], axis=0))
        k0, v0 = pair(0, diag)
        s_all = dot_nt(k0, row_q[s]) * (SCALE * LOG2E)
        dp_all = dot_nt(v0, row_g[s])
        bias = jnp.where(diag == 0, NEG, 0.0).astype(jnp.float32)
        for j in range(PAIR):
            cut = slice(j * BLK, (j + 1) * BLK)
            sc = jnp.concatenate(
                [s_all[:BLK, cut] + bias, jnp.where(causal, s_all[BLK:, cut], NEG)], axis=0
            )
            dp = dp_all[:, cut]
            m = jnp.max(sc, axis=0, keepdims=True)
            e = jnp.exp2(sc - m)
            n = s * PAIR + j
            e_s[0, n] = e
            dp_s[0, n] = dp
            m_s[0, n] = jnp.broadcast_to(m, (8, BLK))
            state += [m, jnp.sum(e, axis=0, keepdims=True), jnp.sum(e * dp, axis=0, keepdims=True)]

    def entry(t, n):
        slot = 2 * (t - 1)
        return slot, cols_ref[step, n * blocks + slot], cols_ref[step, n * blocks + slot + 1]

    def forward(t, state):
        out = []
        for n in range(len(lanes)):
            m, l, u = state[3 * n : 3 * n + 3]
            slot, c1, c2 = entry(t, n)
            count = cnt_ref[step, n]
            b1 = jnp.where(slot < count, 0.0, NEG).astype(jnp.float32)
            b2 = jnp.where(slot + 1 < count, 0.0, NEG).astype(jnp.float32)
            k, v = pair(c1, c2)
            sc = dot_nt(k, qs[n]) * (SCALE * LOG2E)
            sc = jnp.concatenate([sc[:BLK] + b1, sc[BLK:] + b2], axis=0)
            dp = dot_nt(v, gs[n])
            m_new = jnp.maximum(m, jnp.max(sc, axis=0, keepdims=True))
            e = jnp.exp2(sc - m_new)
            alpha = jnp.exp2(m - m_new)
            e_s[t, n] = e
            dp_s[t, n] = dp
            m_s[t, n] = jnp.broadcast_to(m_new, (8, BLK))
            out += [
                m_new,
                l * alpha + jnp.sum(e, axis=0, keepdims=True),
                u * alpha + jnp.sum(e * dp, axis=0, keepdims=True),
            ]
        return tuple(out)

    steps = steps_ref[step, 0]
    state = lax.fori_loop(1, steps, forward, tuple(state))

    top, inv, pull = [], [], []
    for n, (s, j) in enumerate(lanes):
        m, l, u = state[3 * n : 3 * n + 3]
        inv_l = 1.0 / l
        log_norm = m * LN2 + jnp.log(l)
        top.append(m)
        inv.append(inv_l)
        pull.append((2.0 * ZLOSS) * log_norm - u * inv_l)
        z_ref[j : j + 1, :] += log_norm * log_norm

    def weights(t, n):
        factor = jnp.exp2(m_s[t, n][:1] - top[n]) * inv[n]
        probs = e_s[t, n] * factor
        dscore = probs * (dp_s[t, n] + pull[n])
        return probs.astype(jnp.bfloat16), dscore.astype(jnp.bfloat16)

    dk0, dv0 = [], []
    for s in range(ROWS):
        first = [weights(0, s * PAIR + j) for j in range(PAIR)]
        p_all = jnp.concatenate([w[0] for w in first], axis=1)
        d_all = jnp.concatenate([w[1] for w in first], axis=1)
        dk = dot(d_all, row_q[s])
        dv = dot(p_all, row_g[s])
        dk0.append(dk[:BLK])
        dv0.append(dv[:BLK])
        dk_s[diags[s]] += dk[BLK:]
        dv_s[diags[s]] += dv[BLK:]
        dqt = dot(jnp.concatenate([kt_s[0], kt_s[diags[s]]], axis=1), d_all)
        for j in range(PAIR):
            dqt_s[s * PAIR + j] = dqt[:, j * BLK : (j + 1) * BLK]
    dk_s[0] += sum(dk0[1:], dk0[0])
    dv_s[0] += sum(dv0[1:], dv0[0])

    @pl.loop(1, steps)
    def _(t):
        for n in range(len(lanes)):
            _, c1, c2 = entry(t, n)
            p_low, d_low = weights(t, n)
            dk = dot(d_low, qs[n])
            dv = dot(p_low, gs[n])
            dqt_s[n] += dot(jnp.concatenate([kt_s[c1], kt_s[c2]], axis=1), d_low)
            dk_s[c1] += dk[:BLK]
            dv_s[c1] += dv[:BLK]
            dk_s[c2] += dk[BLK:]
            dv_s[c2] += dv[BLK:]

    for n, (s, j) in enumerate(lanes):
        send_ref[ROWS * step + s, :, j * HD : (j + 1) * HD] = (dqt_s[n] * SCALE).T.astype(jnp.bfloat16)

    @pl.when(step == pl.num_programs(0) - 1)
    def _():
        @pl.loop(0, half)
        def _(i):
            mine = core * half + i
            other = (1 - core) * half + i
            send_ref[i, :, 2 * HD : 3 * HD] = (dk_s[mine] * SCALE).astype(jnp.bfloat16)
            send_ref[i, :, 3 * HD :] = dv_s[mine].astype(jnp.bfloat16)
            give_ref[i, :, :HD] = (dk_s[other] * SCALE).astype(jnp.bfloat16)
            give_ref[i, :, HD:] = dv_s[other].astype(jnp.bfloat16)


def attention(recv, mate, cols, cnt, steps, edge):
    half = recv.shape[0]
    blocks = 2 * half
    lanes = ROWS * PAIR
    max_steps = half
    return pl.pallas_call(
        attention_body,
        out_shape=(
            jax.ShapeDtypeStruct((half, BLK, 4 * HD), jnp.bfloat16),
            jax.ShapeDtypeStruct((half, BLK, 2 * HD), jnp.bfloat16),
            jax.ShapeDtypeStruct((Z_ROWS, BLK), jnp.float32),
        ),
        grid_spec=pltpu.PrefetchScalarGridSpec(
            num_scalar_prefetch=4,
            grid=(half // ROWS,),
            in_specs=[
                pl.BlockSpec((ROWS, BLK, 4 * HD), lambda i, *_: (i, 0, 0)),
                pl.BlockSpec(memory_space=pl.ANY),
                pl.BlockSpec(memory_space=pl.ANY),
            ],
            out_specs=[
                pl.BlockSpec((half, BLK, 4 * HD), lambda i, *_: (0, 0, 0)),
                pl.BlockSpec((half, BLK, 2 * HD), lambda i, *_: (0, 0, 0)),
                pl.BlockSpec((Z_ROWS, BLK), lambda i, *_: (0, 0)),
            ],
            scratch_shapes=[
                pltpu.VMEM((blocks, BLK, 2 * HD), jnp.bfloat16),
                pltpu.VMEM((max_steps, lanes, 2 * BLK, BLK), jnp.float32),
                pltpu.VMEM((max_steps, lanes, 2 * BLK, BLK), jnp.float32),
                pltpu.VMEM((max_steps, lanes, 8, BLK), jnp.float32),
                pltpu.VMEM((blocks, BLK, HD), jnp.float32),
                pltpu.VMEM((blocks, BLK, HD), jnp.float32),
                pltpu.VMEM((blocks, HD, BLK), jnp.bfloat16),
                pltpu.VMEM((lanes, HD, BLK), jnp.float32),
                pltpu.SemaphoreType.DMA((2,)),
            ],
        ),
        compiler_params=pltpu.CompilerParams(
            dimension_semantics=("arbitrary",), vmem_limit_bytes=58 << 20
        ),
        cost_estimate=pl.CostEstimate(
            flops=40_000_000_000, transcendentals=4_000_000, bytes_accessed=9_000_000
        ),
        name="block_attention",
    )(cols, cnt, steps, edge, recv, recv, mate)


def pack_body(q_ref, g_ref, k_ref, v_ref, out_ref, hold, in_sem, out_sem):
    chips = out_ref.shape[0]

    def load(p, n):
        ref, width, start, place = (
            (q_ref, 2 * HD, 2 * HD * p, 0),
            (g_ref, 2 * HD, 2 * HD * p, 2 * HD),
            (k_ref, HD, HD * (p // 2), 4 * HD),
            (v_ref, HD, HD * (p // 2), 5 * HD),
        )[n]
        return pltpu.make_async_copy(
            ref.at[0, :, pl.ds(start, width)], hold.at[p, :, pl.ds(place, width)], in_sem.at[p, n]
        )

    loads = [[load(p, n) for n in range(4)] for p in range(chips)]
    stores = [pltpu.make_async_copy(hold.at[p], out_ref.at[p], out_sem.at[p]) for p in range(chips)]
    for four in loads:
        for copy in four:
            copy.start()
    for p in range(chips):
        for copy in loads[p]:
            copy.wait()
        stores[p].start()
    for copy in stores:
        copy.wait()


def pack(queries, out_grad, keys, values):
    tok = queries.shape[1]
    chips = H // PAIR
    shape = (chips, tok, 6 * HD)
    return pl.pallas_call(
        pack_body,
        out_shape=jax.ShapeDtypeStruct(shape, queries.dtype),
        in_specs=[pl.BlockSpec(memory_space=pl.ANY)] * 4,
        out_specs=pl.BlockSpec(memory_space=pl.ANY),
        scratch_shapes=[
            pltpu.VMEM(shape, queries.dtype),
            pltpu.SemaphoreType.DMA((chips, 4)),
            pltpu.SemaphoreType.DMA((chips,)),
        ],
        name="pack",
    )(queries, out_grad, keys, values)


def merge_body(send_ref, got_ref, out_ref, own_s, got_s, in_sem, got_sem, out_sem):
    parts = in_sem.shape[0]
    part = own_s.shape[0] // parts

    def cut(n):
        return pl.ds(n * part, part)

    loads = [
        pltpu.make_async_copy(send_ref.at[cut(n), :, pl.ds(2 * HD, 2 * HD)], own_s.at[cut(n)], in_sem.at[n])
        for n in range(parts)
    ]
    stores = [
        pltpu.make_async_copy(own_s.at[cut(n)], out_ref.at[cut(n), :, pl.ds(2 * HD, 2 * HD)], out_sem.at[n])
        for n in range(parts)
    ]
    gets = [pltpu.make_async_copy(got_ref.at[cut(n)], got_s.at[cut(n)], got_sem.at[n]) for n in range(parts)]
    for n in range(parts):
        loads[n].start()
        gets[n].start()
    for n in range(parts):
        loads[n].wait()
        gets[n].wait()
        rows = slice(n * part, (n + 1) * part)
        both = own_s[rows].astype(jnp.float32) + got_s[rows].astype(jnp.float32)
        own_s[rows] = both.astype(own_s.dtype)
        stores[n].start()
    for copy in stores:
        copy.wait()


def merge(send, got):
    return pl.pallas_call(
        merge_body,
        out_shape=jax.ShapeDtypeStruct(send.shape, send.dtype),
        in_specs=[pl.BlockSpec(memory_space=pl.ANY)] * 2,
        out_specs=pl.BlockSpec(memory_space=pl.ANY),
        scratch_shapes=[
            pltpu.VMEM(got.shape, got.dtype),
            pltpu.VMEM(got.shape, got.dtype),
            pltpu.SemaphoreType.DMA((4,)),
            pltpu.SemaphoreType.DMA((4,)),
            pltpu.SemaphoreType.DMA((4,)),
        ],
        input_output_aliases={0: 0},
        compiler_params=pltpu.CompilerParams(vmem_limit_bytes=60 << 20),
        name="merge",
    )(send, got)


def unpack_body(back_ref, dq_ref, dk_ref, dv_ref, dk_s, dv_s, dq_sem, kv_sem):
    chips = back_ref.shape[0]
    copies = [
        pltpu.make_async_copy(
            back_ref.at[p, :, pl.ds(0, 2 * HD)], dq_ref.at[0, :, pl.ds(p * 2 * HD, 2 * HD)], dq_sem.at[p]
        )
        for p in range(chips)
    ]
    for copy in copies:
        copy.start()
    for g in range(chips // 2):
        both = back_ref[2 * g, :, 2 * HD :].astype(jnp.float32) + back_ref[2 * g + 1, :, 2 * HD :].astype(jnp.float32)
        dk_s[:, g * HD : (g + 1) * HD] = both[:, :HD].astype(dk_s.dtype)
        dv_s[:, g * HD : (g + 1) * HD] = both[:, HD:].astype(dv_s.dtype)
    copies += [
        pltpu.make_async_copy(dk_s, dk_ref.at[0], kv_sem.at[0]),
        pltpu.make_async_copy(dv_s, dv_ref.at[0], kv_sem.at[1]),
    ]
    for copy in copies[chips:]:
        copy.start()
    for copy in copies:
        copy.wait()


def unpack(back):
    chips, tok = back.shape[:2]
    return pl.pallas_call(
        unpack_body,
        out_shape=(
            jax.ShapeDtypeStruct((1, tok, H * HD), back.dtype),
            jax.ShapeDtypeStruct((1, tok, KVH * HD), back.dtype),
            jax.ShapeDtypeStruct((1, tok, KVH * HD), back.dtype),
        ),
        in_specs=[pl.BlockSpec(memory_space=pltpu.VMEM)],
        out_specs=[pl.BlockSpec(memory_space=pl.ANY)] * 3,
        scratch_shapes=[
            pltpu.VMEM((tok, KVH * HD), back.dtype),
            pltpu.VMEM((tok, KVH * HD), back.dtype),
            pltpu.SemaphoreType.DMA((chips,)),
            pltpu.SemaphoreType.DMA((2,)),
        ],
        compiler_params=pltpu.CompilerParams(vmem_limit_bytes=16 << 20),
        name="unpack",
    )(back)


def work_lists(mask, core):
    blocks = mask.shape[2]
    half = blocks // 2
    mask = lax.dynamic_index_in_dim(mask.reshape(PAIR, half, 2, blocks), core, axis=2, keepdims=False)
    mask = jnp.transpose(mask.reshape(PAIR, half // ROWS, ROWS, blocks), (1, 2, 0, 3))
    col = jnp.arange(blocks, dtype=jnp.int32)
    own = (2 * jnp.arange(half, dtype=jnp.int32) + core).reshape(half // ROWS, ROWS)
    other = (mask > 0) & (col > 0) & (col != own[:, :, None, None])
    other = other.astype(jnp.int32).reshape(half // ROWS, ROWS * PAIR, blocks)
    before = (col[None, :] < col[:, None]).astype(jnp.int32)
    rank = jnp.sum(other[:, :, None, :] * before[None, None], axis=3)
    place = col % 2 * half + col // 2
    hit = (rank[:, :, None, :] == col[None, None, :, None]) & (other[:, :, None, :] > 0)
    cols = jnp.sum(jnp.where(hit, place[None, None, None, :], 0), axis=3)
    cnt = jnp.sum(other, axis=2)
    steps = 1 + (jnp.max(cnt, axis=1) + 1) // 2
    edge = jnp.full((1, 3), core, jnp.int32)
    return cols.reshape(half // ROWS, ROWS * PAIR * blocks), cnt, steps[:, None], edge


def body(queries, keys, values, out_grad, block_mask):
    dps = lax.axis_size("dp")
    ctx = lax.axis_size("ctx")
    blocks = block_mask.shape[1]
    me = lax.axis_index("ctx")
    chip, core = me // 2, me % 2
    same = [[2 * p + c for p in range(ctx // 2)] for c in range(2)]
    mates = [(i, i ^ 1) for i in range(ctx)]

    def exchange(a):
        return lax.all_to_all(a, "ctx", 0, 0, axis_index_groups=same, tiled=True)

    mask = lax.dynamic_slice(block_mask, (chip * PAIR, 0, 0), (PAIR, blocks, blocks))
    recv, lists = lax.optimization_barrier(
        (exchange(pack(queries, out_grad, keys, values)), work_lists(mask, core))
    )
    mate = lax.ppermute(recv[:, :, 4 * HD :], "ctx", mates)
    send, give, z = attention(recv, mate, *lists)

    got = lax.ppermute(give, "ctx", mates)
    z_mine = jnp.where(core == 0, z[:1], z[1:2])
    z_mine = z_mine + lax.ppermute(jnp.where(core == 0, z[1:2], z[:1]), "ctx", mates)
    send, z_mine = lax.optimization_barrier((merge(send, got), z_mine))
    back = exchange(send)
    z_own = jnp.sum(lax.all_gather(z_mine, "dp"))[None] * (ZLOSS / (dps * blocks * BLK))
    query_grad, key_grad, value_grad = unpack(back)
    return query_grad, key_grad, value_grad, z_own


def solution(mesh):
    return jax.shard_map(
        body,
        mesh=mesh,
        in_specs=(
            P("dp", "ctx", None),
            P("dp", "ctx", None),
            P("dp", "ctx", None),
            P("dp", "ctx", None),
            P(),
        ),
        out_specs=(P("dp", "ctx", None), P("dp", "ctx", None), P("dp", "ctx", None), P("ctx")),
        check_vma=False,
    )
```

```python
import math

import jax
import jax.numpy as jnp
from jax import lax
from jax.experimental import pallas as pl
from jax.experimental.pallas import tpu as pltpu
from jax.sharding import PartitionSpec as P

H = 32
KVH = 8
HD = 128
BLK = 128
PAIR = 2
ROWS = 4
GROUP = 8
Z_ROWS = 8

ZLOSS = 0.05
NEG = -1e30
LOG2E = 1.0 / math.log(2.0)
LN2 = math.log(2.0)
SCALE = HD ** (-0.5)

NT = (((1,), (1,)), ((), ()))


def attention_body(
    half_ref, lane_ref, groups_ref, edge_ref,
    qd_ref, own_ref, mate_ref,
    send_ref, give_ref, z_ref,
    kv_s, qg_s, e_s, dp_s, m_s, top_s, sum_s, pull_s, dk_s, dv_s, kt_s, dqt_s, sem,
):
    step = pl.program_id(0)
    blocks = kv_s.shape[0]
    half = blocks // 2
    core = edge_ref[0, 2]

    @pl.when(step == 0)
    def _():
        own = pltpu.make_async_copy(
            own_ref.at[:, :, pl.ds(4 * HD, 2 * HD)], kv_s.at[pl.ds(core * half, half)], sem.at[0]
        )
        mate = pltpu.make_async_copy(mate_ref, kv_s.at[pl.ds((1 - core) * half, half)], sem.at[1])
        own.start()
        mate.start()
        dk_s[...] = jnp.zeros_like(dk_s)
        dv_s[...] = jnp.zeros_like(dv_s)
        z_ref[...] = jnp.zeros_like(z_ref)
        own.wait()
        mate.wait()

        @pl.loop(0, blocks // 4)
        def _(b):
            for n in range(4):
                kt_s[4 * b + n] = kv_s[4 * b + n, :, :HD].T

    lanes = [(s, j) for s in range(ROWS) for j in range(PAIR)]
    qs = [qd_ref[s, :, j * HD : (j + 1) * HD] for s, j in lanes]
    gs = [qd_ref[s, :, (PAIR + j) * HD : (PAIR + j + 1) * HD] for s, j in lanes]
    for n in range(len(lanes)):
        qg_s[n, :, :HD] = qs[n]
        qg_s[n, :, HD:] = gs[n]
    base = e_s.shape[0] - len(lanes)

    def wide(x):
        return jnp.broadcast_to(x, (8, BLK))

    def dot(a, b):
        return jnp.dot(a, b, preferred_element_type=jnp.float32)

    def dot_nt(a, b):
        return lax.dot_general(a, b, NT, preferred_element_type=jnp.float32)

    def pair(c1, c2):
        k = jnp.concatenate([kv_s[c1, :, :HD], kv_s[c2, :, :HD]], axis=0)
        v = jnp.concatenate([kv_s[c1, :, HD:], kv_s[c2, :, HD:]], axis=0)
        return k, v

    key_pos = lax.broadcasted_iota(jnp.int32, (BLK, BLK), 0)
    query_pos = lax.broadcasted_iota(jnp.int32, (BLK, BLK), 1)
    causal = key_pos <= query_pos
    row_q, row_g, diags = [], [], []
    for s in range(ROWS):
        diag = core * half + ROWS * step + s
        diags.append(diag)
        row_q.append(jnp.concatenate(qs[s * PAIR : (s + 1) * PAIR], axis=0))
        row_g.append(jnp.concatenate(gs[s * PAIR : (s + 1) * PAIR], axis=0))
        k0, v0 = pair(0, diag)
        s_all = dot_nt(k0, row_q[s]) * (SCALE * LOG2E)
        dp_all = dot_nt(v0, row_g[s])
        bias = jnp.where(diag == 0, NEG, 0.0).astype(jnp.float32)
        for j in range(PAIR):
            cut = slice(j * BLK, (j + 1) * BLK)
            sc = jnp.concatenate(
                [s_all[:BLK, cut] + bias, jnp.where(causal, s_all[BLK:, cut], NEG)], axis=0
            )
            dp = dp_all[:, cut]
            m = jnp.max(sc, axis=0, keepdims=True)
            e = jnp.exp2(sc - m)
            n = s * PAIR + j
            e_s[base + n] = e
            dp_s[base + n] = dp
            m_s[base + n] = wide(m)
            top_s[n] = wide(m)
            sum_s[n] = wide(jnp.sum(e, axis=0, keepdims=True))
            pull_s[n] = wide(jnp.sum(e * dp, axis=0, keepdims=True))

    def entry(i):
        h1, h2 = half_ref[step, 2 * i], half_ref[step, 2 * i + 1]
        return lane_ref[step, i], h1, h2, jnp.maximum(h1 - 1, 0), jnp.maximum(h2 - 1, 0)

    groups = groups_ref[step, 0]

    @pl.loop(0, groups)
    def _(g):
        for k in range(GROUP):
            i = g * GROUP + k
            n, h1, h2, c1, c2 = entry(i)
            b1 = jnp.where(h1 > 0, 0.0, NEG).astype(jnp.float32)
            b2 = jnp.where(h2 > 0, 0.0, NEG).astype(jnp.float32)
            key, value = pair(c1, c2)
            sc = dot_nt(key, qg_s[n, :, :HD]) * (SCALE * LOG2E)
            sc = jnp.concatenate([sc[:BLK] + b1, sc[BLK:] + b2], axis=0)
            dp = dot_nt(value, qg_s[n, :, HD:])
            m = jnp.max(sc, axis=0, keepdims=True)
            e = jnp.exp2(sc - m)
            e_s[i] = e
            dp_s[i] = dp
            m = wide(m)
            m_s[i] = m
            old = top_s[n]
            new = jnp.maximum(old, m)
            keep, take = jnp.exp2(old - new), jnp.exp2(m - new)
            top_s[n] = new
            sum_s[n] = sum_s[n] * keep + wide(jnp.sum(e, axis=0, keepdims=True)) * take
            pull_s[n] = pull_s[n] * keep + wide(jnp.sum(e * dp, axis=0, keepdims=True)) * take

    for n, (s, j) in enumerate(lanes):
        l = sum_s[n]
        inv_l = 1.0 / l
        log_norm = top_s[n] * LN2 + jnp.log(l)
        sum_s[n] = inv_l
        pull_s[n] = (2.0 * ZLOSS) * log_norm - pull_s[n] * inv_l
        z_ref[j : j + 1, :] += log_norm[:1] * log_norm[:1]

    def weights(i, n):
        factor = (jnp.exp2(m_s[i] - top_s[n]) * sum_s[n])[:1]
        probs = e_s[i] * factor
        dscore = probs * (dp_s[i] + pull_s[n][:1])
        return probs.astype(jnp.bfloat16), dscore.astype(jnp.bfloat16)

    dk0, dv0 = [], []
    for s in range(ROWS):
        first = [weights(base + s * PAIR + j, s * PAIR + j) for j in range(PAIR)]
        p_all = jnp.concatenate([w[0] for w in first], axis=1)
        d_all = jnp.concatenate([w[1] for w in first], axis=1)
        dk = dot(d_all, row_q[s])
        dv = dot(p_all, row_g[s])
        dk0.append(dk[:BLK])
        dv0.append(dv[:BLK])
        dk_s[diags[s]] += dk[BLK:]
        dv_s[diags[s]] += dv[BLK:]
        dqt = dot(jnp.concatenate([kt_s[0], kt_s[diags[s]]], axis=1), d_all)
        for j in range(PAIR):
            dqt_s[s * PAIR + j] = dqt[:, j * BLK : (j + 1) * BLK]
    dk_s[0] += sum(dk0[1:], dk0[0])
    dv_s[0] += sum(dv0[1:], dv0[0])

    @pl.loop(0, groups)
    def _(g):
        for k in range(GROUP):
            i = g * GROUP + k
            n, _, _, c1, c2 = entry(i)
            p_low, d_low = weights(i, n)
            dk = dot(d_low, qg_s[n, :, :HD])
            dv = dot(p_low, qg_s[n, :, HD:])
            dqt_s[n] += dot(jnp.concatenate([kt_s[c1], kt_s[c2]], axis=1), d_low)
            dk_s[c1] += dk[:BLK]
            dv_s[c1] += dv[:BLK]
            dk_s[c2] += dk[BLK:]
            dv_s[c2] += dv[BLK:]

    for n, (s, j) in enumerate(lanes):
        send_ref[ROWS * step + s, :, j * HD : (j + 1) * HD] = (dqt_s[n] * SCALE).T.astype(jnp.bfloat16)

    @pl.when(step == pl.num_programs(0) - 1)
    def _():
        @pl.loop(0, half)
        def _(i):
            mine = core * half + i
            other = (1 - core) * half + i
            send_ref[i, :, 2 * HD : 3 * HD] = (dk_s[mine] * SCALE).astype(jnp.bfloat16)
            send_ref[i, :, 3 * HD :] = dv_s[mine].astype(jnp.bfloat16)
            give_ref[i, :, :HD] = (dk_s[other] * SCALE).astype(jnp.bfloat16)
            give_ref[i, :, HD:] = dv_s[other].astype(jnp.bfloat16)


def attention(recv, mate, halves, lane, groups, edge):
    half = recv.shape[0]
    blocks = 2 * half
    lanes = ROWS * PAIR
    items = half * lanes
    return pl.pallas_call(
        attention_body,
        out_shape=(
            jax.ShapeDtypeStruct((half, BLK, 4 * HD), jnp.bfloat16),
            jax.ShapeDtypeStruct((half, BLK, 2 * HD), jnp.bfloat16),
            jax.ShapeDtypeStruct((Z_ROWS, BLK), jnp.float32),
        ),
        grid_spec=pltpu.PrefetchScalarGridSpec(
            num_scalar_prefetch=4,
            grid=(half // ROWS,),
            in_specs=[
                pl.BlockSpec((ROWS, BLK, 4 * HD), lambda i, *_: (i, 0, 0)),
                pl.BlockSpec(memory_space=pl.ANY),
                pl.BlockSpec(memory_space=pl.ANY),
            ],
            out_specs=[
                pl.BlockSpec((half, BLK, 4 * HD), lambda i, *_: (0, 0, 0)),
                pl.BlockSpec((half, BLK, 2 * HD), lambda i, *_: (0, 0, 0)),
                pl.BlockSpec((Z_ROWS, BLK), lambda i, *_: (0, 0)),
            ],
            scratch_shapes=[
                pltpu.VMEM((blocks, BLK, 2 * HD), jnp.bfloat16),
                pltpu.VMEM((lanes, BLK, 2 * HD), jnp.bfloat16),
                pltpu.VMEM((items, 2 * BLK, BLK), jnp.float32),
                pltpu.VMEM((items, 2 * BLK, BLK), jnp.float32),
                pltpu.VMEM((items, 8, BLK), jnp.float32),
                pltpu.VMEM((lanes, 8, BLK), jnp.float32),
                pltpu.VMEM((lanes, 8, BLK), jnp.float32),
                pltpu.VMEM((lanes, 8, BLK), jnp.float32),
                pltpu.VMEM((blocks, BLK, HD), jnp.float32),
                pltpu.VMEM((blocks, BLK, HD), jnp.float32),
                pltpu.VMEM((blocks, HD, BLK), jnp.bfloat16),
                pltpu.VMEM((lanes, HD, BLK), jnp.float32),
                pltpu.SemaphoreType.DMA((2,)),
            ],
        ),
        compiler_params=pltpu.CompilerParams(
            dimension_semantics=("arbitrary",), vmem_limit_bytes=51 << 20
        ),
        cost_estimate=pl.CostEstimate(
            flops=40_000_000_000, transcendentals=4_000_000, bytes_accessed=9_000_000
        ),
        name="block_attention",
    )(halves, lane, groups, edge, recv, recv, mate)


def pack_body(q_ref, g_ref, k_ref, v_ref, out_ref, hold, in_sem, out_sem):
    chips = out_ref.shape[0]

    def load(p, n):
        ref, width, start, place = (
            (q_ref, 2 * HD, 2 * HD * p, 0),
            (g_ref, 2 * HD, 2 * HD * p, 2 * HD),
            (k_ref, HD, HD * (p // 2), 4 * HD),
            (v_ref, HD, HD * (p // 2), 5 * HD),
        )[n]
        return pltpu.make_async_copy(
            ref.at[0, :, pl.ds(start, width)], hold.at[p, :, pl.ds(place, width)], in_sem.at[p, n]
        )

    loads = [[load(p, n) for n in range(4)] for p in range(chips)]
    stores = [pltpu.make_async_copy(hold.at[p], out_ref.at[p], out_sem.at[p]) for p in range(chips)]
    for four in loads:
        for copy in four:
            copy.start()
    for p in range(chips):
        for copy in loads[p]:
            copy.wait()
        stores[p].start()
    for copy in stores:
        copy.wait()


def pack(queries, out_grad, keys, values):
    tok = queries.shape[1]
    chips = H // PAIR
    shape = (chips, tok, 6 * HD)
    return pl.pallas_call(
        pack_body,
        out_shape=jax.ShapeDtypeStruct(shape, queries.dtype),
        in_specs=[pl.BlockSpec(memory_space=pl.ANY)] * 4,
        out_specs=pl.BlockSpec(memory_space=pl.ANY),
        scratch_shapes=[
            pltpu.VMEM(shape, queries.dtype),
            pltpu.SemaphoreType.DMA((chips, 4)),
            pltpu.SemaphoreType.DMA((chips,)),
        ],
        name="pack",
    )(queries, out_grad, keys, values)


def merge_body(send_ref, got_ref, out_ref, own_s, got_s, in_sem, got_sem, out_sem):
    parts = in_sem.shape[0]
    part = own_s.shape[0] // parts

    def cut(n):
        return pl.ds(n * part, part)

    loads = [
        pltpu.make_async_copy(send_ref.at[cut(n), :, pl.ds(2 * HD, 2 * HD)], own_s.at[cut(n)], in_sem.at[n])
        for n in range(parts)
    ]
    stores = [
        pltpu.make_async_copy(own_s.at[cut(n)], out_ref.at[cut(n), :, pl.ds(2 * HD, 2 * HD)], out_sem.at[n])
        for n in range(parts)
    ]
    gets = [pltpu.make_async_copy(got_ref.at[cut(n)], got_s.at[cut(n)], got_sem.at[n]) for n in range(parts)]
    for n in range(parts):
        loads[n].start()
        gets[n].start()
    for n in range(parts):
        loads[n].wait()
        gets[n].wait()
        rows = slice(n * part, (n + 1) * part)
        both = own_s[rows].astype(jnp.float32) + got_s[rows].astype(jnp.float32)
        own_s[rows] = both.astype(own_s.dtype)
        stores[n].start()
    for copy in stores:
        copy.wait()


def merge(send, got):
    return pl.pallas_call(
        merge_body,
        out_shape=jax.ShapeDtypeStruct(send.shape, send.dtype),
        in_specs=[pl.BlockSpec(memory_space=pl.ANY)] * 2,
        out_specs=pl.BlockSpec(memory_space=pl.ANY),
        scratch_shapes=[
            pltpu.VMEM(got.shape, got.dtype),
            pltpu.VMEM(got.shape, got.dtype),
            pltpu.SemaphoreType.DMA((4,)),
            pltpu.SemaphoreType.DMA((4,)),
            pltpu.SemaphoreType.DMA((4,)),
        ],
        input_output_aliases={0: 0},
        compiler_params=pltpu.CompilerParams(vmem_limit_bytes=60 << 20),
        name="merge",
    )(send, got)


def unpack_body(back_ref, dq_ref, dk_ref, dv_ref, dk_s, dv_s, dq_sem, kv_sem):
    chips = back_ref.shape[0]
    copies = [
        pltpu.make_async_copy(
            back_ref.at[p, :, pl.ds(0, 2 * HD)], dq_ref.at[0, :, pl.ds(p * 2 * HD, 2 * HD)], dq_sem.at[p]
        )
        for p in range(chips)
    ]
    for copy in copies:
        copy.start()
    for g in range(chips // 2):
        both = back_ref[2 * g, :, 2 * HD :].astype(jnp.float32) + back_ref[2 * g + 1, :, 2 * HD :].astype(jnp.float32)
        dk_s[:, g * HD : (g + 1) * HD] = both[:, :HD].astype(dk_s.dtype)
        dv_s[:, g * HD : (g + 1) * HD] = both[:, HD:].astype(dv_s.dtype)
    copies += [
        pltpu.make_async_copy(dk_s, dk_ref.at[0], kv_sem.at[0]),
        pltpu.make_async_copy(dv_s, dv_ref.at[0], kv_sem.at[1]),
    ]
    for copy in copies[chips:]:
        copy.start()
    for copy in copies:
        copy.wait()


def unpack(back):
    chips, tok = back.shape[:2]
    return pl.pallas_call(
        unpack_body,
        out_shape=(
            jax.ShapeDtypeStruct((1, tok, H * HD), back.dtype),
            jax.ShapeDtypeStruct((1, tok, KVH * HD), back.dtype),
            jax.ShapeDtypeStruct((1, tok, KVH * HD), back.dtype),
        ),
        in_specs=[pl.BlockSpec(memory_space=pltpu.VMEM)],
        out_specs=[pl.BlockSpec(memory_space=pl.ANY)] * 3,
        scratch_shapes=[
            pltpu.VMEM((tok, KVH * HD), back.dtype),
            pltpu.VMEM((tok, KVH * HD), back.dtype),
            pltpu.SemaphoreType.DMA((chips,)),
            pltpu.SemaphoreType.DMA((2,)),
        ],
        compiler_params=pltpu.CompilerParams(vmem_limit_bytes=16 << 20),
        name="unpack",
    )(back)


def work_lists(mask, core):
    blocks = mask.shape[2]
    half = blocks // 2
    mask = lax.dynamic_index_in_dim(mask.reshape(PAIR, half, 2, blocks), core, axis=2, keepdims=False)
    mask = jnp.transpose(mask.reshape(PAIR, half // ROWS, ROWS, blocks), (1, 2, 0, 3))
    col = jnp.arange(blocks, dtype=jnp.int32)
    own = (2 * jnp.arange(half, dtype=jnp.int32) + core).reshape(half // ROWS, ROWS)
    other = (mask > 0) & (col > 0) & (col != own[:, :, None, None])
    other = other.astype(jnp.int32).reshape(half // ROWS, ROWS * PAIR, blocks)
    lanes = ROWS * PAIR
    before = (col[None, :] < col[:, None]).astype(jnp.int32)
    rank = jnp.sum(other[:, :, None, :] * before[None, None], axis=3)
    pairs = (jnp.sum(other, axis=2) + 1) // 2
    ahead = jnp.arange(lanes, dtype=jnp.int32)
    start = jnp.sum(jnp.where(ahead[None, :] < ahead[:, None], pairs[:, None, :], 0), axis=2)
    slot = jnp.where(other > 0, 2 * start[:, :, None] + rank, -1)
    place = col % 2 * half + col // 2 + 1
    spots = jnp.arange(lanes * blocks, dtype=jnp.int32)
    hit = slot[:, None] == spots[None, :, None, None]
    halves = jnp.sum(jnp.where(hit, place, 0), axis=(2, 3))
    item = jnp.arange(lanes * half, dtype=jnp.int32)
    ends = start + pairs
    lane = jnp.minimum(jnp.sum((ends[:, None, :] <= item[None, :, None]).astype(jnp.int32), axis=2), lanes - 1)
    groups = (jnp.sum(pairs, axis=1, keepdims=True) + GROUP - 1) // GROUP
    edge = jnp.full((1, 3), core, jnp.int32)
    return halves, lane, groups, edge


def body(queries, keys, values, out_grad, block_mask):
    dps = lax.axis_size("dp")
    ctx = lax.axis_size("ctx")
    blocks = block_mask.shape[1]
    me = lax.axis_index("ctx")
    chip, core = me // 2, me % 2
    same = [[2 * p + c for p in range(ctx // 2)] for c in range(2)]
    mates = [(i, i ^ 1) for i in range(ctx)]
    wide = [[d * ctx + 2 * p + c for d in range(dps) for c in range(2)] for p in range(ctx // 2)]

    def exchange(a):
        return lax.all_to_all(a, "ctx", 0, 0, axis_index_groups=same, tiled=True)

    mask = lax.dynamic_slice(block_mask, (chip * PAIR, 0, 0), (PAIR, blocks, blocks))
    recv, lists = lax.optimization_barrier(
        (exchange(pack(queries, out_grad, keys, values)), work_lists(mask, core))
    )
    mate = lax.ppermute(recv[:, :, 4 * HD :], "ctx", mates)
    send, give, z = attention(recv, mate, *lists)

    got = lax.ppermute(give, "ctx", mates)
    send, z = lax.optimization_barrier((merge(send, got), z[:PAIR]))
    back = exchange(send)
    z_all = lax.all_gather(z, ("dp", "ctx"), axis_index_groups=wide)
    z_two = jnp.sum(z_all, axis=(0, 2)) * (ZLOSS / (dps * blocks * BLK))
    z_own = jnp.where(core == 0, z_two[0], z_two[1])[None]
    query_grad, key_grad, value_grad = unpack(back)
    return query_grad, key_grad, value_grad, z_own


def solution(mesh):
    return jax.shard_map(
        body,
        mesh=mesh,
        in_specs=(
            P("dp", "ctx", None),
            P("dp", "ctx", None),
            P("dp", "ctx", None),
            P("dp", "ctx", None),
            P(),
        ),
        out_specs=(P("dp", "ctx", None), P("dp", "ctx", None), P("dp", "ctx", None), P("ctx")),
        check_vma=False,
    )
```

```python
import math

import jax
import jax.numpy as jnp
from jax import lax
from jax.experimental import pallas as pl
from jax.experimental.pallas import tpu as pltpu
from jax.sharding import PartitionSpec as P

H = 32
KVH = 8
HD = 128
BLK = 128
PAIR = 2
ROWS = 4
GROUPS = (8, 4, 2)
Z_ROWS = 8

ZLOSS = 0.05
NEG = -1e30
LOG2E = 1.0 / math.log(2.0)
LN2 = math.log(2.0)
SCALE = HD ** (-0.5)

NT = (((1,), (1,)), ((), ()))


def attention_body(
    half_ref, lane_ref, groups_ref, edge_ref,
    qd_ref, own_ref, mate_ref,
    send_ref, give_ref, z_ref,
    kv_s, qg_s, e_s, dp_s, m_s, top_s, sum_s, pull_s, dk_s, dv_s, kt_s, dqt_s, sem,
):
    step = pl.program_id(0)
    blocks = kv_s.shape[0]
    half = blocks // 2
    core = edge_ref[0, 2]

    @pl.when(step == 0)
    def _():
        own = pltpu.make_async_copy(
            own_ref.at[:, :, pl.ds(4 * HD, 2 * HD)], kv_s.at[pl.ds(core * half, half)], sem.at[0]
        )
        mate = pltpu.make_async_copy(mate_ref, kv_s.at[pl.ds((1 - core) * half, half)], sem.at[1])
        own.start()
        mate.start()
        dk_s[...] = jnp.zeros_like(dk_s)
        dv_s[...] = jnp.zeros_like(dv_s)
        z_ref[...] = jnp.zeros_like(z_ref)
        own.wait()
        mate.wait()

        @pl.loop(0, blocks // 4)
        def _(b):
            for n in range(4):
                kt_s[4 * b + n] = kv_s[4 * b + n, :, :HD].T

    lanes = [(s, j) for s in range(ROWS) for j in range(PAIR)]
    qs = [qd_ref[s, :, j * HD : (j + 1) * HD] for s, j in lanes]
    gs = [qd_ref[s, :, (PAIR + j) * HD : (PAIR + j + 1) * HD] for s, j in lanes]
    for n in range(len(lanes)):
        qg_s[n, :, :HD] = qs[n]
        qg_s[n, :, HD:] = gs[n]
    base = e_s.shape[0] - len(lanes)

    def wide(x):
        return jnp.broadcast_to(x, (8, BLK))

    def dot(a, b):
        return jnp.dot(a, b, preferred_element_type=jnp.float32)

    def dot_nt(a, b):
        return lax.dot_general(a, b, NT, preferred_element_type=jnp.float32)

    def pair(c1, c2):
        k = jnp.concatenate([kv_s[c1, :, :HD], kv_s[c2, :, :HD]], axis=0)
        v = jnp.concatenate([kv_s[c1, :, HD:], kv_s[c2, :, HD:]], axis=0)
        return k, v

    key_pos = lax.broadcasted_iota(jnp.int32, (BLK, BLK), 0)
    query_pos = lax.broadcasted_iota(jnp.int32, (BLK, BLK), 1)
    causal = key_pos <= query_pos
    row_q, row_g, diags = [], [], []
    for s in range(ROWS):
        diag = core * half + ROWS * step + s
        diags.append(diag)
        row_q.append(jnp.concatenate(qs[s * PAIR : (s + 1) * PAIR], axis=0))
        row_g.append(jnp.concatenate(gs[s * PAIR : (s + 1) * PAIR], axis=0))
        k0, v0 = pair(0, diag)
        s_all = dot_nt(k0, row_q[s]) * (SCALE * LOG2E)
        dp_all = dot_nt(v0, row_g[s])
        bias = jnp.where(diag == 0, NEG, 0.0).astype(jnp.float32)
        for j in range(PAIR):
            cut = slice(j * BLK, (j + 1) * BLK)
            sc = jnp.concatenate(
                [s_all[:BLK, cut] + bias, jnp.where(causal, s_all[BLK:, cut], NEG)], axis=0
            )
            dp = dp_all[:, cut]
            m = jnp.max(sc, axis=0, keepdims=True)
            e = jnp.exp2(sc - m)
            n = s * PAIR + j
            e_s[base + n] = e
            dp_s[base + n] = dp
            m_s[base + n] = wide(m)
            top_s[n] = wide(m)
            sum_s[n] = wide(jnp.sum(e, axis=0, keepdims=True))
            pull_s[n] = wide(jnp.sum(e * dp, axis=0, keepdims=True))

    def entry(i):
        h1, h2 = half_ref[step, 2 * i], half_ref[step, 2 * i + 1]
        return lane_ref[step, i], h1, h2, jnp.maximum(h1 - 1, 0), jnp.maximum(h2 - 1, 0)

    def over_items(one):
        done = 0
        for n, size in enumerate(GROUPS):
            count = groups_ref[step, n]

            @pl.loop(0, count)
            def _(g, done=done, size=size):
                for k in range(size):
                    one(done + g * size + k)

            done = done + count * size

    @over_items
    def _(i):
        n, h1, h2, c1, c2 = entry(i)
        b1 = jnp.where(h1 > 0, 0.0, NEG).astype(jnp.float32)
        b2 = jnp.where(h2 > 0, 0.0, NEG).astype(jnp.float32)
        key, value = pair(c1, c2)
        sc = dot_nt(key, qg_s[n, :, :HD]) * (SCALE * LOG2E)
        sc = jnp.concatenate([sc[:BLK] + b1, sc[BLK:] + b2], axis=0)
        dp = dot_nt(value, qg_s[n, :, HD:])
        m = jnp.max(sc, axis=0, keepdims=True)
        e = jnp.exp2(sc - m)
        e_s[i] = e
        dp_s[i] = dp
        m = wide(m)
        m_s[i] = m
        old = top_s[n]
        new = jnp.maximum(old, m)
        keep, take = jnp.exp2(old - new), jnp.exp2(m - new)
        top_s[n] = new
        sum_s[n] = sum_s[n] * keep + wide(jnp.sum(e, axis=0, keepdims=True)) * take
        pull_s[n] = pull_s[n] * keep + wide(jnp.sum(e * dp, axis=0, keepdims=True)) * take

    for n, (s, j) in enumerate(lanes):
        l = sum_s[n]
        inv_l = 1.0 / l
        log_norm = top_s[n] * LN2 + jnp.log(l)
        sum_s[n] = inv_l
        pull_s[n] = (2.0 * ZLOSS) * log_norm - pull_s[n] * inv_l
        z_ref[j : j + 1, :] += log_norm[:1] * log_norm[:1]

    def weights(i, n):
        factor = (jnp.exp2(m_s[i] - top_s[n]) * sum_s[n])[:1]
        probs = e_s[i] * factor
        dscore = probs * (dp_s[i] + pull_s[n][:1])
        return probs.astype(jnp.bfloat16), dscore.astype(jnp.bfloat16)

    dk0, dv0 = [], []
    for s in range(ROWS):
        first = [weights(base + s * PAIR + j, s * PAIR + j) for j in range(PAIR)]
        p_all = jnp.concatenate([w[0] for w in first], axis=1)
        d_all = jnp.concatenate([w[1] for w in first], axis=1)
        dk = dot(d_all, row_q[s])
        dv = dot(p_all, row_g[s])
        dk0.append(dk[:BLK])
        dv0.append(dv[:BLK])
        dk_s[diags[s]] += dk[BLK:]
        dv_s[diags[s]] += dv[BLK:]
        dqt = dot(jnp.concatenate([kt_s[0], kt_s[diags[s]]], axis=1), d_all)
        for j in range(PAIR):
            dqt_s[s * PAIR + j] = dqt[:, j * BLK : (j + 1) * BLK]
    dk_s[0] += sum(dk0[1:], dk0[0])
    dv_s[0] += sum(dv0[1:], dv0[0])

    @over_items
    def _(i):
        n, _, _, c1, c2 = entry(i)
        p_low, d_low = weights(i, n)
        dk = dot(d_low, qg_s[n, :, :HD])
        dv = dot(p_low, qg_s[n, :, HD:])
        dqt_s[n] += dot(jnp.concatenate([kt_s[c1], kt_s[c2]], axis=1), d_low)
        dk_s[c1] += dk[:BLK]
        dv_s[c1] += dv[:BLK]
        dk_s[c2] += dk[BLK:]
        dv_s[c2] += dv[BLK:]

    for n, (s, j) in enumerate(lanes):
        send_ref[ROWS * step + s, :, j * HD : (j + 1) * HD] = (dqt_s[n] * SCALE).T.astype(jnp.bfloat16)

    @pl.when(step == pl.num_programs(0) - 1)
    def _():
        @pl.loop(0, half)
        def _(i):
            mine = core * half + i
            other = (1 - core) * half + i
            send_ref[i, :, 2 * HD : 3 * HD] = (dk_s[mine] * SCALE).astype(jnp.bfloat16)
            send_ref[i, :, 3 * HD :] = dv_s[mine].astype(jnp.bfloat16)
            give_ref[i, :, :HD] = (dk_s[other] * SCALE).astype(jnp.bfloat16)
            give_ref[i, :, HD:] = dv_s[other].astype(jnp.bfloat16)


def attention(recv, mate, halves, lane, groups, edge):
    half = recv.shape[0]
    blocks = 2 * half
    lanes = ROWS * PAIR
    items = half * lanes
    return pl.pallas_call(
        attention_body,
        out_shape=(
            jax.ShapeDtypeStruct((half, BLK, 4 * HD), jnp.bfloat16),
            jax.ShapeDtypeStruct((half, BLK, 2 * HD), jnp.bfloat16),
            jax.ShapeDtypeStruct((Z_ROWS, BLK), jnp.float32),
        ),
        grid_spec=pltpu.PrefetchScalarGridSpec(
            num_scalar_prefetch=4,
            grid=(half // ROWS,),
            in_specs=[
                pl.BlockSpec((ROWS, BLK, 4 * HD), lambda i, *_: (i, 0, 0)),
                pl.BlockSpec(memory_space=pl.ANY),
                pl.BlockSpec(memory_space=pl.ANY),
            ],
            out_specs=[
                pl.BlockSpec((half, BLK, 4 * HD), lambda i, *_: (0, 0, 0)),
                pl.BlockSpec((half, BLK, 2 * HD), lambda i, *_: (0, 0, 0)),
                pl.BlockSpec((Z_ROWS, BLK), lambda i, *_: (0, 0)),
            ],
            scratch_shapes=[
                pltpu.VMEM((blocks, BLK, 2 * HD), jnp.bfloat16),
                pltpu.VMEM((lanes, BLK, 2 * HD), jnp.bfloat16),
                pltpu.VMEM((items, 2 * BLK, BLK), jnp.float32),
                pltpu.VMEM((items, 2 * BLK, BLK), jnp.float32),
                pltpu.VMEM((items, 8, BLK), jnp.float32),
                pltpu.VMEM((lanes, 8, BLK), jnp.float32),
                pltpu.VMEM((lanes, 8, BLK), jnp.float32),
                pltpu.VMEM((lanes, 8, BLK), jnp.float32),
                pltpu.VMEM((blocks, BLK, HD), jnp.float32),
                pltpu.VMEM((blocks, BLK, HD), jnp.float32),
                pltpu.VMEM((blocks, HD, BLK), jnp.bfloat16),
                pltpu.VMEM((lanes, HD, BLK), jnp.float32),
                pltpu.SemaphoreType.DMA((2,)),
            ],
        ),
        compiler_params=pltpu.CompilerParams(
            dimension_semantics=("arbitrary",), vmem_limit_bytes=51 << 20
        ),
        cost_estimate=pl.CostEstimate(
            flops=40_000_000_000, transcendentals=4_000_000, bytes_accessed=9_000_000
        ),
        name="block_attention",
    )(halves, lane, groups, edge, recv, recv, mate)


def pack_body(q_ref, g_ref, k_ref, v_ref, out_ref, hold, in_sem, out_sem):
    chips = out_ref.shape[0]

    def load(p, n):
        ref, width, start, place = (
            (q_ref, 2 * HD, 2 * HD * p, 0),
            (g_ref, 2 * HD, 2 * HD * p, 2 * HD),
            (k_ref, HD, HD * (p // 2), 4 * HD),
            (v_ref, HD, HD * (p // 2), 5 * HD),
        )[n]
        return pltpu.make_async_copy(
            ref.at[0, :, pl.ds(start, width)], hold.at[p, :, pl.ds(place, width)], in_sem.at[p, n]
        )

    loads = [[load(p, n) for n in range(4)] for p in range(chips)]
    stores = [pltpu.make_async_copy(hold.at[p], out_ref.at[p], out_sem.at[p]) for p in range(chips)]
    for four in loads:
        for copy in four:
            copy.start()
    for p in range(chips):
        for copy in loads[p]:
            copy.wait()
        stores[p].start()
    for copy in stores:
        copy.wait()


def pack(queries, out_grad, keys, values):
    tok = queries.shape[1]
    chips = H // PAIR
    shape = (chips, tok, 6 * HD)
    return pl.pallas_call(
        pack_body,
        out_shape=jax.ShapeDtypeStruct(shape, queries.dtype),
        in_specs=[pl.BlockSpec(memory_space=pl.ANY)] * 4,
        out_specs=pl.BlockSpec(memory_space=pl.ANY),
        scratch_shapes=[
            pltpu.VMEM(shape, queries.dtype),
            pltpu.SemaphoreType.DMA((chips, 4)),
            pltpu.SemaphoreType.DMA((chips,)),
        ],
        name="pack",
    )(queries, out_grad, keys, values)


def merge_body(send_ref, got_ref, out_ref, own_s, got_s, in_sem, got_sem, out_sem):
    parts = in_sem.shape[0]
    part = own_s.shape[0] // parts

    def cut(n):
        return pl.ds(n * part, part)

    loads = [
        pltpu.make_async_copy(send_ref.at[cut(n), :, pl.ds(2 * HD, 2 * HD)], own_s.at[cut(n)], in_sem.at[n])
        for n in range(parts)
    ]
    stores = [
        pltpu.make_async_copy(own_s.at[cut(n)], out_ref.at[cut(n), :, pl.ds(2 * HD, 2 * HD)], out_sem.at[n])
        for n in range(parts)
    ]
    gets = [pltpu.make_async_copy(got_ref.at[cut(n)], got_s.at[cut(n)], got_sem.at[n]) for n in range(parts)]
    for n in range(parts):
        loads[n].start()
        gets[n].start()
    for n in range(parts):
        loads[n].wait()
        gets[n].wait()
        rows = slice(n * part, (n + 1) * part)
        both = own_s[rows].astype(jnp.float32) + got_s[rows].astype(jnp.float32)
        own_s[rows] = both.astype(own_s.dtype)
        stores[n].start()
    for copy in stores:
        copy.wait()


def merge(send, got):
    return pl.pallas_call(
        merge_body,
        out_shape=jax.ShapeDtypeStruct(send.shape, send.dtype),
        in_specs=[pl.BlockSpec(memory_space=pl.ANY)] * 2,
        out_specs=pl.BlockSpec(memory_space=pl.ANY),
        scratch_shapes=[
            pltpu.VMEM(got.shape, got.dtype),
            pltpu.VMEM(got.shape, got.dtype),
            pltpu.SemaphoreType.DMA((4,)),
            pltpu.SemaphoreType.DMA((4,)),
            pltpu.SemaphoreType.DMA((4,)),
        ],
        input_output_aliases={0: 0},
        compiler_params=pltpu.CompilerParams(vmem_limit_bytes=60 << 20),
        name="merge",
    )(send, got)


def unpack_body(back_ref, dq_ref, dk_ref, dv_ref, dk_s, dv_s, dq_sem, kv_sem):
    chips = back_ref.shape[0]
    copies = [
        pltpu.make_async_copy(
            back_ref.at[p, :, pl.ds(0, 2 * HD)], dq_ref.at[0, :, pl.ds(p * 2 * HD, 2 * HD)], dq_sem.at[p]
        )
        for p in range(chips)
    ]
    for copy in copies:
        copy.start()
    for g in range(chips // 2):
        both = back_ref[2 * g, :, 2 * HD :].astype(jnp.float32) + back_ref[2 * g + 1, :, 2 * HD :].astype(jnp.float32)
        dk_s[:, g * HD : (g + 1) * HD] = both[:, :HD].astype(dk_s.dtype)
        dv_s[:, g * HD : (g + 1) * HD] = both[:, HD:].astype(dv_s.dtype)
    copies += [
        pltpu.make_async_copy(dk_s, dk_ref.at[0], kv_sem.at[0]),
        pltpu.make_async_copy(dv_s, dv_ref.at[0], kv_sem.at[1]),
    ]
    for copy in copies[chips:]:
        copy.start()
    for copy in copies:
        copy.wait()


def unpack(back):
    chips, tok = back.shape[:2]
    return pl.pallas_call(
        unpack_body,
        out_shape=(
            jax.ShapeDtypeStruct((1, tok, H * HD), back.dtype),
            jax.ShapeDtypeStruct((1, tok, KVH * HD), back.dtype),
            jax.ShapeDtypeStruct((1, tok, KVH * HD), back.dtype),
        ),
        in_specs=[pl.BlockSpec(memory_space=pltpu.VMEM)],
        out_specs=[pl.BlockSpec(memory_space=pl.ANY)] * 3,
        scratch_shapes=[
            pltpu.VMEM((tok, KVH * HD), back.dtype),
            pltpu.VMEM((tok, KVH * HD), back.dtype),
            pltpu.SemaphoreType.DMA((chips,)),
            pltpu.SemaphoreType.DMA((2,)),
        ],
        compiler_params=pltpu.CompilerParams(vmem_limit_bytes=16 << 20),
        name="unpack",
    )(back)


def work_lists(mask, core):
    blocks = mask.shape[2]
    half = blocks // 2
    mask = lax.dynamic_index_in_dim(mask.reshape(PAIR, half, 2, blocks), core, axis=2, keepdims=False)
    mask = jnp.transpose(mask.reshape(PAIR, half // ROWS, ROWS, blocks), (1, 2, 0, 3))
    col = jnp.arange(blocks, dtype=jnp.int32)
    own = (2 * jnp.arange(half, dtype=jnp.int32) + core).reshape(half // ROWS, ROWS)
    other = (mask > 0) & (col > 0) & (col != own[:, :, None, None])
    other = other.astype(jnp.int32).reshape(half // ROWS, ROWS * PAIR, blocks)
    lanes = ROWS * PAIR
    before = (col[None, :] < col[:, None]).astype(jnp.int32)
    rank = jnp.sum(other[:, :, None, :] * before[None, None], axis=3)
    pairs = (jnp.sum(other, axis=2) + 1) // 2
    ahead = jnp.arange(lanes, dtype=jnp.int32)
    start = jnp.sum(jnp.where(ahead[None, :] < ahead[:, None], pairs[:, None, :], 0), axis=2)
    slot = jnp.where(other > 0, 2 * start[:, :, None] + rank, -1)
    place = col % 2 * half + col // 2 + 1
    spots = jnp.arange(lanes * blocks, dtype=jnp.int32)
    hit = slot[:, None] == spots[None, :, None, None]
    halves = jnp.sum(jnp.where(hit, place, 0), axis=(2, 3))
    item = jnp.arange(lanes * half, dtype=jnp.int32)
    ends = start + pairs
    lane = jnp.minimum(jnp.sum((ends[:, None, :] <= item[None, :, None]).astype(jnp.int32), axis=2), lanes - 1)
    left = jnp.sum(pairs, axis=1)
    groups = []
    for size, spare in zip(GROUPS, GROUPS[1:] + (1,)):
        count = (left + size - 1 - spare * (spare > 1)) // size
        groups.append(jnp.maximum(count, 0))
        left = jnp.maximum(left - count * size, 0)
    groups = jnp.stack(groups, axis=1)
    edge = jnp.full((1, 3), core, jnp.int32)
    return halves, lane, groups, edge


def body(queries, keys, values, out_grad, block_mask):
    dps = lax.axis_size("dp")
    ctx = lax.axis_size("ctx")
    blocks = block_mask.shape[1]
    me = lax.axis_index("ctx")
    chip, core = me // 2, me % 2
    same = [[2 * p + c for p in range(ctx // 2)] for c in range(2)]
    mates = [(i, i ^ 1) for i in range(ctx)]
    wide = [[d * ctx + 2 * p + c for d in range(dps) for c in range(2)] for p in range(ctx // 2)]

    def exchange(a):
        return lax.all_to_all(a, "ctx", 0, 0, axis_index_groups=same, tiled=True)

    mask = lax.dynamic_slice(block_mask, (chip * PAIR, 0, 0), (PAIR, blocks, blocks))
    recv, lists = lax.optimization_barrier(
        (exchange(pack(queries, out_grad, keys, values)), work_lists(mask, core))
    )
    mate = lax.ppermute(recv[:, :, 4 * HD :], "ctx", mates)
    send, give, z = attention(recv, mate, *lists)

    got = lax.ppermute(give, "ctx", mates)
    send, z = lax.optimization_barrier((merge(send, got), z[:PAIR]))
    back = exchange(send)
    z_all = lax.all_gather(z, ("dp", "ctx"), axis_index_groups=wide)
    z_two = jnp.sum(z_all, axis=(0, 2)) * (ZLOSS / (dps * blocks * BLK))
    z_own = jnp.where(core == 0, z_two[0], z_two[1])[None]
    query_grad, key_grad, value_grad = unpack(back)
    return query_grad, key_grad, value_grad, z_own


def solution(mesh):
    return jax.shard_map(
        body,
        mesh=mesh,
        in_specs=(
            P("dp", "ctx", None),
            P("dp", "ctx", None),
            P("dp", "ctx", None),
            P("dp", "ctx", None),
            P(),
        ),
        out_specs=(P("dp", "ctx", None), P("dp", "ctx", None), P("dp", "ctx", None), P("ctx")),
        check_vma=False,
    )
```

```python
import math

import jax
import jax.numpy as jnp
from jax import lax
from jax.experimental import pallas as pl
from jax.experimental.pallas import tpu as pltpu
from jax.sharding import PartitionSpec as P

H = 32
KVH = 8
HD = 128
BLK = 128
PAIR = 2
ROWS = 4
GROUPS = (8, 4, 2)
Z_ROWS = 8

ZLOSS = 0.05
NEG = -1e30
LOG2E = 1.0 / math.log(2.0)
LN2 = math.log(2.0)
SCALE = HD ** (-0.5)

NT = (((1,), (1,)), ((), ()))


def attention_body(
    half_ref, lane_ref, groups_ref, edge_ref,
    qd_ref, own_ref, mate_ref,
    send_ref, give_ref, z_ref,
    kv_s, qg_s, e_s, dp_s, m_s, top_s, sum_s, pull_s, dk_s, dv_s, kt_s, dqt_s, sem,
):
    step = pl.program_id(0)
    blocks = kv_s.shape[0]
    half = blocks // 2
    core = edge_ref[0, 2]

    @pl.when(step == 0)
    def _():
        own = pltpu.make_async_copy(
            own_ref.at[:, :, pl.ds(4 * HD, 2 * HD)], kv_s.at[pl.ds(core * half, half)], sem.at[0]
        )
        mate = pltpu.make_async_copy(mate_ref, kv_s.at[pl.ds((1 - core) * half, half)], sem.at[1])
        own.start()
        mate.start()
        dk_s[...] = jnp.zeros_like(dk_s)
        dv_s[...] = jnp.zeros_like(dv_s)
        z_ref[...] = jnp.zeros_like(z_ref)
        own.wait()
        mate.wait()

        @pl.loop(0, blocks // 4)
        def _(b):
            for n in range(4):
                kt_s[4 * b + n] = kv_s[4 * b + n, :, :HD].T

    lanes = [(s, j) for s in range(ROWS) for j in range(PAIR)]
    qs = [qd_ref[s, :, j * HD : (j + 1) * HD] for s, j in lanes]
    gs = [qd_ref[s, :, (PAIR + j) * HD : (PAIR + j + 1) * HD] for s, j in lanes]
    for n in range(len(lanes)):
        qg_s[n, :, :HD] = qs[n]
        qg_s[n, :, HD:] = gs[n]
    base = e_s.shape[0] - len(lanes)

    def wide(x):
        return jnp.broadcast_to(x, (8, BLK))

    def dot(a, b):
        return jnp.dot(a, b, preferred_element_type=jnp.float32)

    def dot_nt(a, b):
        return lax.dot_general(a, b, NT, preferred_element_type=jnp.float32)

    def pair(c1, c2):
        k = jnp.concatenate([kv_s[c1, :, :HD], kv_s[c2, :, :HD]], axis=0)
        v = jnp.concatenate([kv_s[c1, :, HD:], kv_s[c2, :, HD:]], axis=0)
        return k, v

    key_pos = lax.broadcasted_iota(jnp.int32, (BLK, BLK), 0)
    query_pos = lax.broadcasted_iota(jnp.int32, (BLK, BLK), 1)
    causal = key_pos <= query_pos
    row_q, row_g, diags = [], [], []
    for s in range(ROWS):
        diag = core * half + ROWS * step + s
        diags.append(diag)
        row_q.append(jnp.concatenate(qs[s * PAIR : (s + 1) * PAIR], axis=0))
        row_g.append(jnp.concatenate(gs[s * PAIR : (s + 1) * PAIR], axis=0))
        k0, v0 = pair(0, diag)
        s_all = dot_nt(k0, row_q[s]) * (SCALE * LOG2E)
        dp_all = dot_nt(v0, row_g[s])
        bias = jnp.where(diag == 0, NEG, 0.0).astype(jnp.float32)
        for j in range(PAIR):
            cut = slice(j * BLK, (j + 1) * BLK)
            sc = jnp.concatenate(
                [s_all[:BLK, cut] + bias, jnp.where(causal, s_all[BLK:, cut], NEG)], axis=0
            )
            dp = dp_all[:, cut]
            m = jnp.max(sc, axis=0, keepdims=True)
            e = jnp.exp2(sc - m)
            n = s * PAIR + j
            e_s[base + n] = e
            dp_s[base + n] = dp
            m_s[base + n] = wide(m)
            top_s[n] = wide(m)
            sum_s[n] = wide(jnp.sum(e, axis=0, keepdims=True))
            pull_s[n] = wide(jnp.sum(e * dp, axis=0, keepdims=True))

    def entry(i):
        h1, h2 = half_ref[step, 2 * i], half_ref[step, 2 * i + 1]
        return lane_ref[step, i], h1, h2, jnp.maximum(h1 - 1, 0), jnp.maximum(h2 - 1, 0)

    def over_items(one):
        done = 0
        for n, size in enumerate(GROUPS):
            count = groups_ref[step, n]

            @pl.loop(0, count)
            def _(g, done=done, size=size):
                for k in range(size):
                    one(done + g * size + k)

            done = done + count * size

    @over_items
    def _(i):
        n, h1, h2, c1, c2 = entry(i)
        b1 = jnp.where(h1 > 0, 0.0, NEG).astype(jnp.float32)
        b2 = jnp.where(h2 > 0, 0.0, NEG).astype(jnp.float32)
        key, value = pair(c1, c2)
        sc = dot_nt(key, qg_s[n, :, :HD]) * (SCALE * LOG2E)
        sc = jnp.concatenate([sc[:BLK] + b1, sc[BLK:] + b2], axis=0)
        dp = dot_nt(value, qg_s[n, :, HD:])
        m = jnp.max(sc, axis=0, keepdims=True)
        e = jnp.exp2(sc - m)
        e_s[i] = e
        dp_s[i] = dp
        m = wide(m)
        m_s[i] = m
        old = top_s[n]
        new = jnp.maximum(old, m)
        keep, take = jnp.exp2(old - new), jnp.exp2(m - new)
        top_s[n] = new
        sum_s[n] = sum_s[n] * keep + wide(jnp.sum(e, axis=0, keepdims=True)) * take
        pull_s[n] = pull_s[n] * keep + wide(jnp.sum(e * dp, axis=0, keepdims=True)) * take

    for n, (s, j) in enumerate(lanes):
        l = sum_s[n]
        inv_l = 1.0 / l
        log_norm = top_s[n] * LN2 + jnp.log(l)
        sum_s[n] = inv_l
        pull_s[n] = (2.0 * ZLOSS) * log_norm - pull_s[n] * inv_l
        z_ref[j : j + 1, :] += log_norm[:1] * log_norm[:1]

    def weights(i, n):
        factor = (jnp.exp2(m_s[i] - top_s[n]) * sum_s[n])[:1]
        probs = e_s[i] * factor
        dscore = probs * (dp_s[i] + pull_s[n][:1])
        return probs.astype(jnp.bfloat16), dscore.astype(jnp.bfloat16)

    dk0, dv0 = [], []
    for s in range(ROWS):
        first = [weights(base + s * PAIR + j, s * PAIR + j) for j in range(PAIR)]
        p_all = jnp.concatenate([w[0] for w in first], axis=1)
        d_all = jnp.concatenate([w[1] for w in first], axis=1)
        dk = dot(d_all, row_q[s])
        dv = dot(p_all, row_g[s])
        dk0.append(dk[:BLK])
        dv0.append(dv[:BLK])
        dk_s[diags[s]] += dk[BLK:]
        dv_s[diags[s]] += dv[BLK:]
        dqt = dot(jnp.concatenate([kt_s[0], kt_s[diags[s]]], axis=1), d_all)
        for j in range(PAIR):
            dqt_s[s * PAIR + j] = dqt[:, j * BLK : (j + 1) * BLK]
    dk_s[0] += sum(dk0[1:], dk0[0])
    dv_s[0] += sum(dv0[1:], dv0[0])

    @over_items
    def _(i):
        n, _, _, c1, c2 = entry(i)
        p_low, d_low = weights(i, n)
        dk = dot(d_low, qg_s[n, :, :HD])
        dv = dot(p_low, qg_s[n, :, HD:])
        dqt_s[n] += dot(jnp.concatenate([kt_s[c1], kt_s[c2]], axis=1), d_low)
        dk_s[c1] += dk[:BLK]
        dv_s[c1] += dv[:BLK]
        dk_s[c2] += dk[BLK:]
        dv_s[c2] += dv[BLK:]

    for n, (s, j) in enumerate(lanes):
        send_ref[ROWS * step + s, :, j * HD : (j + 1) * HD] = (dqt_s[n] * SCALE).T.astype(jnp.bfloat16)

    @pl.when(step == pl.num_programs(0) - 1)
    def _():
        @pl.loop(0, half)
        def _(i):
            mine = core * half + i
            other = (1 - core) * half + i
            send_ref[i, :, 2 * HD : 3 * HD] = (dk_s[mine] * SCALE).astype(jnp.bfloat16)
            send_ref[i, :, 3 * HD :] = dv_s[mine].astype(jnp.bfloat16)
            give_ref[i, :, :HD] = (dk_s[other] * SCALE).astype(jnp.bfloat16)
            give_ref[i, :, HD:] = dv_s[other].astype(jnp.bfloat16)


def attention(recv, mate, halves, lane, groups, edge):
    half = recv.shape[0]
    blocks = 2 * half
    lanes = ROWS * PAIR
    items = half * lanes
    return pl.pallas_call(
        attention_body,
        out_shape=(
            jax.ShapeDtypeStruct((half, BLK, 4 * HD), jnp.bfloat16),
            jax.ShapeDtypeStruct((half, BLK, 2 * HD), jnp.bfloat16),
            jax.ShapeDtypeStruct((Z_ROWS, BLK), jnp.float32),
        ),
        grid_spec=pltpu.PrefetchScalarGridSpec(
            num_scalar_prefetch=4,
            grid=(half // ROWS,),
            in_specs=[
                pl.BlockSpec((ROWS, BLK, 4 * HD), lambda i, *_: (i, 0, 0)),
                pl.BlockSpec(memory_space=pl.ANY),
                pl.BlockSpec(memory_space=pl.ANY),
            ],
            out_specs=[
                pl.BlockSpec((half, BLK, 4 * HD), lambda i, *_: (0, 0, 0)),
                pl.BlockSpec((half, BLK, 2 * HD), lambda i, *_: (0, 0, 0)),
                pl.BlockSpec((Z_ROWS, BLK), lambda i, *_: (0, 0)),
            ],
            scratch_shapes=[
                pltpu.VMEM((blocks, BLK, 2 * HD), jnp.bfloat16),
                pltpu.VMEM((lanes, BLK, 2 * HD), jnp.bfloat16),
                pltpu.VMEM((items, 2 * BLK, BLK), jnp.float32),
                pltpu.VMEM((items, 2 * BLK, BLK), jnp.float32),
                pltpu.VMEM((items, 8, BLK), jnp.float32),
                pltpu.VMEM((lanes, 8, BLK), jnp.float32),
                pltpu.VMEM((lanes, 8, BLK), jnp.float32),
                pltpu.VMEM((lanes, 8, BLK), jnp.float32),
                pltpu.VMEM((blocks, BLK, HD), jnp.float32),
                pltpu.VMEM((blocks, BLK, HD), jnp.float32),
                pltpu.VMEM((blocks, HD, BLK), jnp.bfloat16),
                pltpu.VMEM((lanes, HD, BLK), jnp.float32),
                pltpu.SemaphoreType.DMA((2,)),
            ],
        ),
        compiler_params=pltpu.CompilerParams(
            dimension_semantics=("arbitrary",), vmem_limit_bytes=51 << 20
        ),
        cost_estimate=pl.CostEstimate(
            flops=40_000_000_000, transcendentals=4_000_000, bytes_accessed=9_000_000
        ),
        name="block_attention",
    )(halves, lane, groups, edge, recv, recv, mate)


def pack_body(q_ref, g_ref, k_ref, v_ref, out_ref, hold, in_sem, out_sem):
    chips = out_ref.shape[0]

    def load(p, n):
        ref, width, start, place = (
            (q_ref, 2 * HD, 2 * HD * p, 0),
            (g_ref, 2 * HD, 2 * HD * p, 2 * HD),
            (k_ref, HD, HD * (p // 2), 4 * HD),
            (v_ref, HD, HD * (p // 2), 5 * HD),
        )[n]
        return pltpu.make_async_copy(
            ref.at[0, :, pl.ds(start, width)], hold.at[p, :, pl.ds(place, width)], in_sem.at[p, n]
        )

    loads = [[load(p, n) for n in range(4)] for p in range(chips)]
    stores = [pltpu.make_async_copy(hold.at[p], out_ref.at[p], out_sem.at[p]) for p in range(chips)]
    for four in loads:
        for copy in four:
            copy.start()
    for p in range(chips):
        for copy in loads[p]:
            copy.wait()
        stores[p].start()
    for copy in stores:
        copy.wait()


def pack(queries, out_grad, keys, values):
    tok = queries.shape[1]
    chips = H // PAIR
    shape = (chips, tok, 6 * HD)
    return pl.pallas_call(
        pack_body,
        out_shape=jax.ShapeDtypeStruct(shape, queries.dtype),
        in_specs=[pl.BlockSpec(memory_space=pl.ANY)] * 4,
        out_specs=pl.BlockSpec(memory_space=pl.ANY),
        scratch_shapes=[
            pltpu.VMEM(shape, queries.dtype),
            pltpu.SemaphoreType.DMA((chips, 4)),
            pltpu.SemaphoreType.DMA((chips,)),
        ],
        name="pack",
    )(queries, out_grad, keys, values)


def merge_body(send_ref, got_ref, out_ref, own_s, in_sem, out_sem):
    parts = in_sem.shape[0]
    part = own_s.shape[0] // parts

    def cut(n):
        return pl.ds(n * part, part)

    loads = [
        pltpu.make_async_copy(send_ref.at[cut(n), :, pl.ds(2 * HD, 2 * HD)], own_s.at[cut(n)], in_sem.at[n])
        for n in range(parts)
    ]
    stores = [
        pltpu.make_async_copy(own_s.at[cut(n)], out_ref.at[cut(n), :, pl.ds(2 * HD, 2 * HD)], out_sem.at[n])
        for n in range(parts)
    ]
    for n in range(parts):
        loads[n].start()
    for n in range(parts):
        loads[n].wait()
        rows = slice(n * part, (n + 1) * part)
        both = own_s[rows].astype(jnp.float32) + got_ref[rows].astype(jnp.float32)
        own_s[rows] = both.astype(own_s.dtype)
        stores[n].start()
    for copy in stores:
        copy.wait()


def merge(send, got):
    return pl.pallas_call(
        merge_body,
        out_shape=jax.ShapeDtypeStruct(send.shape, send.dtype),
        in_specs=[pl.BlockSpec(memory_space=pl.ANY), pl.BlockSpec(memory_space=pltpu.VMEM)],
        out_specs=pl.BlockSpec(memory_space=pl.ANY),
        scratch_shapes=[
            pltpu.VMEM(got.shape, got.dtype),
            pltpu.SemaphoreType.DMA((4,)),
            pltpu.SemaphoreType.DMA((4,)),
        ],
        input_output_aliases={0: 0},
        compiler_params=pltpu.CompilerParams(vmem_limit_bytes=52 << 20),
        name="merge",
    )(send, got)


def unpack_body(back_ref, dq_ref, dk_ref, dv_ref, dk_s, dv_s, dq_sem, kv_sem):
    chips = back_ref.shape[0]
    copies = [
        pltpu.make_async_copy(
            back_ref.at[p, :, pl.ds(0, 2 * HD)], dq_ref.at[0, :, pl.ds(p * 2 * HD, 2 * HD)], dq_sem.at[p]
        )
        for p in range(chips)
    ]
    for copy in copies:
        copy.start()
    for g in range(chips // 2):
        both = back_ref[2 * g, :, 2 * HD :].astype(jnp.float32) + back_ref[2 * g + 1, :, 2 * HD :].astype(jnp.float32)
        dk_s[:, g * HD : (g + 1) * HD] = both[:, :HD].astype(dk_s.dtype)
        dv_s[:, g * HD : (g + 1) * HD] = both[:, HD:].astype(dv_s.dtype)
    copies += [
        pltpu.make_async_copy(dk_s, dk_ref.at[0], kv_sem.at[0]),
        pltpu.make_async_copy(dv_s, dv_ref.at[0], kv_sem.at[1]),
    ]
    for copy in copies[chips:]:
        copy.start()
    for copy in copies:
        copy.wait()


def unpack(back):
    chips, tok = back.shape[:2]
    return pl.pallas_call(
        unpack_body,
        out_shape=(
            jax.ShapeDtypeStruct((1, tok, H * HD), back.dtype),
            jax.ShapeDtypeStruct((1, tok, KVH * HD), back.dtype),
            jax.ShapeDtypeStruct((1, tok, KVH * HD), back.dtype),
        ),
        in_specs=[pl.BlockSpec(memory_space=pltpu.VMEM)],
        out_specs=[pl.BlockSpec(memory_space=pl.ANY)] * 3,
        scratch_shapes=[
            pltpu.VMEM((tok, KVH * HD), back.dtype),
            pltpu.VMEM((tok, KVH * HD), back.dtype),
            pltpu.SemaphoreType.DMA((chips,)),
            pltpu.SemaphoreType.DMA((2,)),
        ],
        compiler_params=pltpu.CompilerParams(vmem_limit_bytes=16 << 20),
        name="unpack",
    )(back)


def work_lists(mask, core):
    blocks = mask.shape[2]
    half = blocks // 2
    mask = lax.dynamic_index_in_dim(mask.reshape(PAIR, half, 2, blocks), core, axis=2, keepdims=False)
    mask = jnp.transpose(mask.reshape(PAIR, half // ROWS, ROWS, blocks), (1, 2, 0, 3))
    col = jnp.arange(blocks, dtype=jnp.int32)
    own = (2 * jnp.arange(half, dtype=jnp.int32) + core).reshape(half // ROWS, ROWS)
    other = (mask > 0) & (col > 0) & (col != own[:, :, None, None])
    other = other.astype(jnp.int32).reshape(half // ROWS, ROWS * PAIR, blocks)
    lanes = ROWS * PAIR
    before = (col[None, :] < col[:, None]).astype(jnp.int32)
    rank = jnp.sum(other[:, :, None, :] * before[None, None], axis=3)
    pairs = (jnp.sum(other, axis=2) + 1) // 2
    ahead = jnp.arange(lanes, dtype=jnp.int32)
    start = jnp.sum(jnp.where(ahead[None, :] < ahead[:, None], pairs[:, None, :], 0), axis=2)
    slot = jnp.where(other > 0, 2 * start[:, :, None] + rank, -1)
    place = col % 2 * half + col // 2 + 1
    spots = jnp.arange(lanes * blocks, dtype=jnp.int32)
    hit = slot[:, None] == spots[None, :, None, None]
    halves = jnp.sum(jnp.where(hit, place, 0), axis=(2, 3))
    item = jnp.arange(lanes * half, dtype=jnp.int32)
    ends = start + pairs
    lane = jnp.minimum(jnp.sum((ends[:, None, :] <= item[None, :, None]).astype(jnp.int32), axis=2), lanes - 1)
    left = jnp.sum(pairs, axis=1)
    groups = []
    for size, spare in zip(GROUPS, GROUPS[1:] + (1,)):
        count = (left + size - 1 - spare * (spare > 1)) // size
        groups.append(jnp.maximum(count, 0))
        left = jnp.maximum(left - count * size, 0)
    groups = jnp.stack(groups, axis=1)
    edge = jnp.full((1, 3), core, jnp.int32)
    return halves, lane, groups, edge


def body(queries, keys, values, out_grad, block_mask):
    dps = lax.axis_size("dp")
    ctx = lax.axis_size("ctx")
    blocks = block_mask.shape[1]
    me = lax.axis_index("ctx")
    chip, core = me // 2, me % 2
    same = [[2 * p + c for p in range(ctx // 2)] for c in range(2)]
    mates = [(i, i ^ 1) for i in range(ctx)]
    wide = [[d * ctx + 2 * p + c for d in range(dps) for c in range(2)] for p in range(ctx // 2)]

    def exchange(a):
        return lax.all_to_all(a, "ctx", 0, 0, axis_index_groups=same, tiled=True)

    mask = lax.dynamic_slice(block_mask, (chip * PAIR, 0, 0), (PAIR, blocks, blocks))
    recv, lists = lax.optimization_barrier(
        (exchange(pack(queries, out_grad, keys, values)), work_lists(mask, core))
    )
    mate = lax.ppermute(recv[:, :, 4 * HD :], "ctx", mates)
    send, give, z = attention(recv, mate, *lists)

    got = lax.ppermute(give, "ctx", mates)
    send, z = lax.optimization_barrier((merge(send, got), z[:PAIR]))
    back = exchange(send)
    z_all = lax.all_gather(z, ("dp", "ctx"), axis_index_groups=wide)
    z_two = jnp.sum(z_all, axis=(0, 2)) * (ZLOSS / (dps * blocks * BLK))
    z_own = jnp.where(core == 0, z_two[0], z_two[1])[None]
    query_grad, key_grad, value_grad = unpack(back)
    return query_grad, key_grad, value_grad, z_own


def solution(mesh):
    return jax.shard_map(
        body,
        mesh=mesh,
        in_specs=(
            P("dp", "ctx", None),
            P("dp", "ctx", None),
            P("dp", "ctx", None),
            P("dp", "ctx", None),
            P(),
        ),
        out_specs=(P("dp", "ctx", None), P("dp", "ctx", None), P("dp", "ctx", None), P("ctx")),
        check_vma=False,
    )
```

```python
import math

import jax
import jax.numpy as jnp
from jax import lax
from jax.experimental import pallas as pl
from jax.experimental.pallas import tpu as pltpu
from jax.sharding import PartitionSpec as P

H = 32
KVH = 8
HD = 128
BLK = 128
PAIR = 2
ROWS = 4
GROUPS = (16, 8, 4)
Z_ROWS = 8

ZLOSS = 0.05
NEG = -1e30
LOG2E = 1.0 / math.log(2.0)
LN2 = math.log(2.0)
SCALE = HD ** (-0.5)

NT = (((1,), (1,)), ((), ()))


def attention_body(
    half_ref, lane_ref, groups_ref, edge_ref,
    qd_ref, own_ref, mate_ref,
    send_ref, give_ref, z_ref,
    kv_s, qg_s, e_s, dp_s, m_s, top_s, sum_s, pull_s, dk_s, dv_s, kt_s, dqt_s, sem,
):
    step = pl.program_id(0)
    blocks = kv_s.shape[0]
    half = blocks // 2
    core = edge_ref[0, 2]

    @pl.when(step == 0)
    def _():
        own = pltpu.make_async_copy(
            own_ref.at[:, :, pl.ds(4 * HD, 2 * HD)], kv_s.at[pl.ds(core * half, half)], sem.at[0]
        )
        mate = pltpu.make_async_copy(mate_ref, kv_s.at[pl.ds((1 - core) * half, half)], sem.at[1])
        own.start()
        mate.start()
        dk_s[...] = jnp.zeros_like(dk_s)
        dv_s[...] = jnp.zeros_like(dv_s)
        z_ref[...] = jnp.zeros_like(z_ref)
        own.wait()
        mate.wait()

        @pl.loop(0, blocks // 4)
        def _(b):
            for n in range(4):
                kt_s[4 * b + n] = kv_s[4 * b + n, :, :HD].T

    lanes = [(s, j) for s in range(ROWS) for j in range(PAIR)]
    qs = [qd_ref[s, :, j * HD : (j + 1) * HD] for s, j in lanes]
    gs = [qd_ref[s, :, (PAIR + j) * HD : (PAIR + j + 1) * HD] for s, j in lanes]
    for n in range(len(lanes)):
        qg_s[n, :, :HD] = qs[n]
        qg_s[n, :, HD:] = gs[n]
    base = e_s.shape[0] - len(lanes)

    def wide(x):
        return jnp.broadcast_to(x, (8, BLK))

    def dot(a, b):
        return jnp.dot(a, b, preferred_element_type=jnp.float32)

    def dot_nt(a, b):
        return lax.dot_general(a, b, NT, preferred_element_type=jnp.float32)

    def pair(c1, c2):
        k = jnp.concatenate([kv_s[c1, :, :HD], kv_s[c2, :, :HD]], axis=0)
        v = jnp.concatenate([kv_s[c1, :, HD:], kv_s[c2, :, HD:]], axis=0)
        return k, v

    key_pos = lax.broadcasted_iota(jnp.int32, (BLK, BLK), 0)
    query_pos = lax.broadcasted_iota(jnp.int32, (BLK, BLK), 1)
    causal = key_pos <= query_pos
    row_q, row_g, diags = [], [], []
    for s in range(ROWS):
        diag = core * half + ROWS * step + s
        diags.append(diag)
        row_q.append(jnp.concatenate(qs[s * PAIR : (s + 1) * PAIR], axis=0))
        row_g.append(jnp.concatenate(gs[s * PAIR : (s + 1) * PAIR], axis=0))
        k0, v0 = pair(0, diag)
        s_all = dot_nt(k0, row_q[s]) * (SCALE * LOG2E)
        dp_all = dot_nt(v0, row_g[s])
        bias = jnp.where(diag == 0, NEG, 0.0).astype(jnp.float32)
        for j in range(PAIR):
            cut = slice(j * BLK, (j + 1) * BLK)
            sc = jnp.concatenate(
                [s_all[:BLK, cut] + bias, jnp.where(causal, s_all[BLK:, cut], NEG)], axis=0
            )
            dp = dp_all[:, cut]
            m = jnp.max(sc, axis=0, keepdims=True)
            e = jnp.exp2(sc - m)
            n = s * PAIR + j
            e_s[base + n] = e
            dp_s[base + n] = dp
            m_s[base + n] = wide(m)
            top_s[n] = wide(m)
            sum_s[n] = wide(jnp.sum(e, axis=0, keepdims=True))
            pull_s[n] = wide(jnp.sum(e * dp, axis=0, keepdims=True))

    def entry(i):
        h1, h2 = half_ref[step, 2 * i], half_ref[step, 2 * i + 1]
        return lane_ref[step, i], h1, h2, jnp.maximum(h1 - 1, 0), jnp.maximum(h2 - 1, 0)

    def over_items(one):
        done = 0
        for n, size in enumerate(GROUPS):
            count = groups_ref[step, n]

            @pl.loop(0, count)
            def _(g, done=done, size=size):
                for k in range(size):
                    one(done + g * size + k)

            done = done + count * size

    @over_items
    def _(i):
        n, h1, h2, c1, c2 = entry(i)
        b1 = jnp.where(h1 > 0, 0.0, NEG).astype(jnp.float32)
        b2 = jnp.where(h2 > 0, 0.0, NEG).astype(jnp.float32)
        key, value = pair(c1, c2)
        sc = dot_nt(key, qg_s[n, :, :HD]) * (SCALE * LOG2E)
        sc = jnp.concatenate([sc[:BLK] + b1, sc[BLK:] + b2], axis=0)
        dp = dot_nt(value, qg_s[n, :, HD:])
        m = jnp.max(sc, axis=0, keepdims=True)
        e = jnp.exp2(sc - m)
        e_s[i] = e
        dp_s[i] = dp
        m = wide(m)
        m_s[i] = m
        old = top_s[n]
        new = jnp.maximum(old, m)
        keep, take = jnp.exp2(old - new), jnp.exp2(m - new)
        top_s[n] = new
        sum_s[n] = sum_s[n] * keep + wide(jnp.sum(e, axis=0, keepdims=True)) * take
        pull_s[n] = pull_s[n] * keep + wide(jnp.sum(e * dp, axis=0, keepdims=True)) * take

    for n, (s, j) in enumerate(lanes):
        l = sum_s[n]
        inv_l = 1.0 / l
        log_norm = top_s[n] * LN2 + jnp.log(l)
        sum_s[n] = inv_l
        pull_s[n] = (2.0 * ZLOSS) * log_norm - pull_s[n] * inv_l
        z_ref[j : j + 1, :] += log_norm[:1] * log_norm[:1]

    def weights(i, n):
        factor = (jnp.exp2(m_s[i] - top_s[n]) * sum_s[n])[:1]
        probs = e_s[i] * factor
        dscore = probs * (dp_s[i] + pull_s[n][:1])
        return probs.astype(jnp.bfloat16), dscore.astype(jnp.bfloat16)

    dk0, dv0 = [], []
    for s in range(ROWS):
        first = [weights(base + s * PAIR + j, s * PAIR + j) for j in range(PAIR)]
        p_all = jnp.concatenate([w[0] for w in first], axis=1)
        d_all = jnp.concatenate([w[1] for w in first], axis=1)
        dk = dot(d_all, row_q[s])
        dv = dot(p_all, row_g[s])
        dk0.append(dk[:BLK])
        dv0.append(dv[:BLK])
        dk_s[diags[s]] += dk[BLK:]
        dv_s[diags[s]] += dv[BLK:]
        dqt = dot(jnp.concatenate([kt_s[0], kt_s[diags[s]]], axis=1), d_all)
        for j in range(PAIR):
            dqt_s[s * PAIR + j] = dqt[:, j * BLK : (j + 1) * BLK]
    dk_s[0] += sum(dk0[1:], dk0[0])
    dv_s[0] += sum(dv0[1:], dv0[0])

    @over_items
    def _(i):
        n, _, _, c1, c2 = entry(i)
        p_low, d_low = weights(i, n)
        dk = dot(d_low, qg_s[n, :, :HD])
        dv = dot(p_low, qg_s[n, :, HD:])
        dqt_s[n] += dot(jnp.concatenate([kt_s[c1], kt_s[c2]], axis=1), d_low)
        dk_s[c1] += dk[:BLK]
        dv_s[c1] += dv[:BLK]
        dk_s[c2] += dk[BLK:]
        dv_s[c2] += dv[BLK:]

    for n, (s, j) in enumerate(lanes):
        send_ref[ROWS * step + s, :, j * HD : (j + 1) * HD] = (dqt_s[n] * SCALE).T.astype(jnp.bfloat16)

    @pl.when(step == pl.num_programs(0) - 1)
    def _():
        @pl.loop(0, half)
        def _(i):
            mine = core * half + i
            other = (1 - core) * half + i
            send_ref[i, :, 2 * HD : 3 * HD] = (dk_s[mine] * SCALE).astype(jnp.bfloat16)
            send_ref[i, :, 3 * HD :] = dv_s[mine].astype(jnp.bfloat16)
            give_ref[i, :, :HD] = (dk_s[other] * SCALE).astype(jnp.bfloat16)
            give_ref[i, :, HD:] = dv_s[other].astype(jnp.bfloat16)


def attention(recv, mate, halves, lane, groups, edge):
    half = recv.shape[0]
    blocks = 2 * half
    lanes = ROWS * PAIR
    items = half * lanes
    return pl.pallas_call(
        attention_body,
        out_shape=(
            jax.ShapeDtypeStruct((half, BLK, 4 * HD), jnp.bfloat16),
            jax.ShapeDtypeStruct((half, BLK, 2 * HD), jnp.bfloat16),
            jax.ShapeDtypeStruct((Z_ROWS, BLK), jnp.float32),
        ),
        grid_spec=pltpu.PrefetchScalarGridSpec(
            num_scalar_prefetch=4,
            grid=(half // ROWS,),
            in_specs=[
                pl.BlockSpec((ROWS, BLK, 4 * HD), lambda i, *_: (i, 0, 0)),
                pl.BlockSpec(memory_space=pl.ANY),
                pl.BlockSpec(memory_space=pl.ANY),
            ],
            out_specs=[
                pl.BlockSpec((half, BLK, 4 * HD), lambda i, *_: (0, 0, 0)),
                pl.BlockSpec((half, BLK, 2 * HD), lambda i, *_: (0, 0, 0)),
                pl.BlockSpec((Z_ROWS, BLK), lambda i, *_: (0, 0)),
            ],
            scratch_shapes=[
                pltpu.VMEM((blocks, BLK, 2 * HD), jnp.bfloat16),
                pltpu.VMEM((lanes, BLK, 2 * HD), jnp.bfloat16),
                pltpu.VMEM((items, 2 * BLK, BLK), jnp.float32),
                pltpu.VMEM((items, 2 * BLK, BLK), jnp.float32),
                pltpu.VMEM((items, 8, BLK), jnp.float32),
                pltpu.VMEM((lanes, 8, BLK), jnp.float32),
                pltpu.VMEM((lanes, 8, BLK), jnp.float32),
                pltpu.VMEM((lanes, 8, BLK), jnp.float32),
                pltpu.VMEM((blocks, BLK, HD), jnp.float32),
                pltpu.VMEM((blocks, BLK, HD), jnp.float32),
                pltpu.VMEM((blocks, HD, BLK), jnp.bfloat16),
                pltpu.VMEM((lanes, HD, BLK), jnp.float32),
                pltpu.SemaphoreType.DMA((2,)),
            ],
        ),
        compiler_params=pltpu.CompilerParams(
            dimension_semantics=("arbitrary",), vmem_limit_bytes=51 << 20
        ),
        cost_estimate=pl.CostEstimate(
            flops=40_000_000_000, transcendentals=4_000_000, bytes_accessed=9_000_000
        ),
        name="block_attention",
    )(halves, lane, groups, edge, recv, recv, mate)


def pack_body(q_ref, g_ref, k_ref, v_ref, out_ref, hold, in_sem, out_sem):
    chips = out_ref.shape[0]

    def load(p, n):
        ref, width, start, place = (
            (q_ref, 2 * HD, 2 * HD * p, 0),
            (g_ref, 2 * HD, 2 * HD * p, 2 * HD),
            (k_ref, HD, HD * (p // 2), 4 * HD),
            (v_ref, HD, HD * (p // 2), 5 * HD),
        )[n]
        return pltpu.make_async_copy(
            ref.at[0, :, pl.ds(start, width)], hold.at[p, :, pl.ds(place, width)], in_sem.at[p, n]
        )

    loads = [[load(p, n) for n in range(4)] for p in range(chips)]
    stores = [pltpu.make_async_copy(hold.at[p], out_ref.at[p], out_sem.at[p]) for p in range(chips)]
    for four in loads:
        for copy in four:
            copy.start()
    for p in range(chips):
        for copy in loads[p]:
            copy.wait()
        stores[p].start()
    for copy in stores:
        copy.wait()


def pack(queries, out_grad, keys, values):
    tok = queries.shape[1]
    chips = H // PAIR
    shape = (chips, tok, 6 * HD)
    return pl.pallas_call(
        pack_body,
        out_shape=jax.ShapeDtypeStruct(shape, queries.dtype),
        in_specs=[pl.BlockSpec(memory_space=pl.ANY)] * 4,
        out_specs=pl.BlockSpec(memory_space=pl.ANY),
        scratch_shapes=[
            pltpu.VMEM(shape, queries.dtype),
            pltpu.SemaphoreType.DMA((chips, 4)),
            pltpu.SemaphoreType.DMA((chips,)),
        ],
        name="pack",
    )(queries, out_grad, keys, values)


def merge_body(send_ref, got_ref, out_ref, own_s, in_sem, out_sem):
    parts = in_sem.shape[0]
    part = own_s.shape[0] // parts

    def cut(n):
        return pl.ds(n * part, part)

    loads = [
        pltpu.make_async_copy(send_ref.at[cut(n), :, pl.ds(2 * HD, 2 * HD)], own_s.at[cut(n)], in_sem.at[n])
        for n in range(parts)
    ]
    stores = [
        pltpu.make_async_copy(own_s.at[cut(n)], out_ref.at[cut(n), :, pl.ds(2 * HD, 2 * HD)], out_sem.at[n])
        for n in range(parts)
    ]
    for n in range(parts):
        loads[n].start()
    for n in range(parts):
        loads[n].wait()
        rows = slice(n * part, (n + 1) * part)
        both = own_s[rows].astype(jnp.float32) + got_ref[rows].astype(jnp.float32)
        own_s[rows] = both.astype(own_s.dtype)
        stores[n].start()
    for copy in stores:
        copy.wait()


def merge(send, got):
    return pl.pallas_call(
        merge_body,
        out_shape=jax.ShapeDtypeStruct(send.shape, send.dtype),
        in_specs=[pl.BlockSpec(memory_space=pl.ANY), pl.BlockSpec(memory_space=pltpu.VMEM)],
        out_specs=pl.BlockSpec(memory_space=pl.ANY),
        scratch_shapes=[
            pltpu.VMEM(got.shape, got.dtype),
            pltpu.SemaphoreType.DMA((4,)),
            pltpu.SemaphoreType.DMA((4,)),
        ],
        input_output_aliases={0: 0},
        compiler_params=pltpu.CompilerParams(vmem_limit_bytes=52 << 20),
        name="merge",
    )(send, got)


def unpack_body(back_ref, dq_ref, dk_ref, dv_ref, dk_s, dv_s, dq_sem, kv_sem):
    chips = back_ref.shape[0]
    copies = [
        pltpu.make_async_copy(
            back_ref.at[p, :, pl.ds(0, 2 * HD)], dq_ref.at[0, :, pl.ds(p * 2 * HD, 2 * HD)], dq_sem.at[p]
        )
        for p in range(chips)
    ]
    for copy in copies:
        copy.start()
    for g in range(chips // 2):
        both = back_ref[2 * g, :, 2 * HD :].astype(jnp.float32) + back_ref[2 * g + 1, :, 2 * HD :].astype(jnp.float32)
        dk_s[:, g * HD : (g + 1) * HD] = both[:, :HD].astype(dk_s.dtype)
        dv_s[:, g * HD : (g + 1) * HD] = both[:, HD:].astype(dv_s.dtype)
    copies += [
        pltpu.make_async_copy(dk_s, dk_ref.at[0], kv_sem.at[0]),
        pltpu.make_async_copy(dv_s, dv_ref.at[0], kv_sem.at[1]),
    ]
    for copy in copies[chips:]:
        copy.start()
    for copy in copies:
        copy.wait()


def unpack(back):
    chips, tok = back.shape[:2]
    return pl.pallas_call(
        unpack_body,
        out_shape=(
            jax.ShapeDtypeStruct((1, tok, H * HD), back.dtype),
            jax.ShapeDtypeStruct((1, tok, KVH * HD), back.dtype),
            jax.ShapeDtypeStruct((1, tok, KVH * HD), back.dtype),
        ),
        in_specs=[pl.BlockSpec(memory_space=pltpu.VMEM)],
        out_specs=[pl.BlockSpec(memory_space=pl.ANY)] * 3,
        scratch_shapes=[
            pltpu.VMEM((tok, KVH * HD), back.dtype),
            pltpu.VMEM((tok, KVH * HD), back.dtype),
            pltpu.SemaphoreType.DMA((chips,)),
            pltpu.SemaphoreType.DMA((2,)),
        ],
        compiler_params=pltpu.CompilerParams(vmem_limit_bytes=16 << 20),
        name="unpack",
    )(back)


def work_lists(mask, core):
    blocks = mask.shape[2]
    half = blocks // 2
    mask = lax.dynamic_index_in_dim(mask.reshape(PAIR, half, 2, blocks), core, axis=2, keepdims=False)
    mask = jnp.transpose(mask.reshape(PAIR, half // ROWS, ROWS, blocks), (1, 2, 0, 3))
    col = jnp.arange(blocks, dtype=jnp.int32)
    own = (2 * jnp.arange(half, dtype=jnp.int32) + core).reshape(half // ROWS, ROWS)
    other = (mask > 0) & (col > 0) & (col != own[:, :, None, None])
    other = other.astype(jnp.int32).reshape(half // ROWS, ROWS * PAIR, blocks)
    lanes = ROWS * PAIR
    before = (col[None, :] < col[:, None]).astype(jnp.int32)
    rank = jnp.sum(other[:, :, None, :] * before[None, None], axis=3)
    pairs = (jnp.sum(other, axis=2) + 1) // 2
    ahead = jnp.arange(lanes, dtype=jnp.int32)
    start = jnp.sum(jnp.where(ahead[None, :] < ahead[:, None], pairs[:, None, :], 0), axis=2)
    slot = jnp.where(other > 0, 2 * start[:, :, None] + rank, -1)
    place = col % 2 * half + col // 2 + 1
    spots = jnp.arange(lanes * blocks, dtype=jnp.int32)
    hit = slot[:, None] == spots[None, :, None, None]
    halves = jnp.sum(jnp.where(hit, place, 0), axis=(2, 3))
    item = jnp.arange(lanes * half, dtype=jnp.int32)
    ends = start + pairs
    lane = jnp.minimum(jnp.sum((ends[:, None, :] <= item[None, :, None]).astype(jnp.int32), axis=2), lanes - 1)
    left = jnp.sum(pairs, axis=1)
    groups = []
    for size, spare in zip(GROUPS, GROUPS[1:] + (1,)):
        count = (left + size - 1 - spare * (spare > 1)) // size
        groups.append(jnp.maximum(count, 0))
        left = jnp.maximum(left - count * size, 0)
    groups = jnp.stack(groups, axis=1)
    edge = jnp.full((1, 3), core, jnp.int32)
    return halves, lane, groups, edge


def body(queries, keys, values, out_grad, block_mask):
    dps = lax.axis_size("dp")
    ctx = lax.axis_size("ctx")
    blocks = block_mask.shape[1]
    me = lax.axis_index("ctx")
    chip, core = me // 2, me % 2
    same = [[2 * p + c for p in range(ctx // 2)] for c in range(2)]
    mates = [(i, i ^ 1) for i in range(ctx)]
    wide = [[d * ctx + 2 * p + c for d in range(dps) for c in range(2)] for p in range(ctx // 2)]

    def exchange(a):
        return lax.all_to_all(a, "ctx", 0, 0, axis_index_groups=same, tiled=True)

    mask = lax.dynamic_slice(block_mask, (chip * PAIR, 0, 0), (PAIR, blocks, blocks))
    recv, lists = lax.optimization_barrier(
        (exchange(pack(queries, out_grad, keys, values)), work_lists(mask, core))
    )
    mate = lax.ppermute(recv[:, :, 4 * HD :], "ctx", mates)
    send, give, z = attention(recv, mate, *lists)

    got = lax.ppermute(give, "ctx", mates)
    send, z = lax.optimization_barrier((merge(send, got), z[:PAIR]))
    back = exchange(send)
    z_all = lax.all_gather(z, ("dp", "ctx"), axis_index_groups=wide)
    z_two = jnp.sum(z_all, axis=(0, 2)) * (ZLOSS / (dps * blocks * BLK))
    z_own = jnp.where(core == 0, z_two[0], z_two[1])[None]
    query_grad, key_grad, value_grad = unpack(back)
    return query_grad, key_grad, value_grad, z_own


def solution(mesh):
    return jax.shard_map(
        body,
        mesh=mesh,
        in_specs=(
            P("dp", "ctx", None),
            P("dp", "ctx", None),
            P("dp", "ctx", None),
            P("dp", "ctx", None),
            P(),
        ),
        out_specs=(P("dp", "ctx", None), P("dp", "ctx", None), P("dp", "ctx", None), P("ctx")),
        check_vma=False,
    )
```
